256 devices in a mesh: dp: 32 (over x, z), seq: 8 (over y, core).
Axes of the slice: x: 4, y: 4, z: 8, core: 2. Of those that a mesh axis runs over, the one named last changes fastest.
Arguments:
- words: bfloat16 [128, 1024, 1024], P('dp', 'seq'), may hold values from -6 to 6
- patches: bfloat16 [128, 2048, 1024], P('dp', 'seq'), may hold values from -6 to 6
- proj: bfloat16 [1024, 1024], P('dp'), may hold values from -0.1875 to 0.1875
- routes: int32 [128, 1024, 1], P('dp', 'seq'), may hold values from 0 to 7; in each aligned block of 128 rows (0 to 127, 128 to 255, ..., all dimensions but the last counted through in order) at most 32 rows name the same one
- targets: int32 [128, 1024], P('dp', 'seq'), may hold values from 0 to 255
- counts: int32 [128], P('dp'), may hold values from 512 to 1024
- flags: int32 [128, 16, 32], P('dp'), may hold values 0 or 1
Outputs:
- word_loss: float32 [128, 1024], P('dp', 'seq')
- proj_grad: float32 [1024, 1024], P('dp', 'seq')
The draws below stay inside these ranges and needn't reach their ends.
Inputs may be any that keep to these rules, and one draw needn't show every extreme that they name: `routes`: among the 128 words of one page held by one index of seq, at most 32 name the same shard; some block reaches 32.
All inputs are finite; a program needn't handle non-finite values. No bound on the sum of `flags` on one device may be relied on, other than what follows from the above.
Results may differ from the reference program's by a relative error of at most 0.0065.
Values may be sent and summed in bfloat16 or wider, within the bound.
A program may use at most 64 MiB of HBM per device.

```python
import math
import jax
import jax.numpy as jnp
import numpy as np
from jax import lax

D = 1024
P_SIZE = 2048
PAGE_WORD_SLOTS = 1024
MARGIN_BLOCK_SIZE = 64
PAGES = 128
W_DEV = 128
PPS = 256
CAP = 32
WB = 16
PB = 32
N_SEQ = 8


def draw_counts(key, part):
    drawn = jax.random.randint(key, (PAGES,), PAGE_WORD_SLOTS // 2, PAGE_WORD_SLOTS + 1, dtype=jnp.int32)
    return drawn.at[0].set(PAGE_WORD_SLOTS)


def with_ends(values, key, least, top_value):
    longest = values.shape.index(max(values.shape))
    spots = []
    for shift in (0, 1):
        where = [jax.random.randint(jax.random.fold_in(key, axis), (), 0, length) for axis, length in enumerate(values.shape)]
        where[longest] = (where[longest] + shift) % values.shape[longest]
        spots.append(tuple(where))
    return values.at[spots[0]].set(least).at[spots[1]].set(top_value)


def spiked(values, stream_key, source, target, blocks, factor):
    def block_of(position):
        return (jnp.arange(values.shape[position]) // (values.shape[position] // blocks)).reshape((-1,) + (1,) * (values.ndim - 1 - position))

    one_side = jax.random.permutation(stream_key, blocks)[block_of(target)]
    second = (block_of(target) + blocks // 2) % blocks
    return jnp.where((block_of(source) == one_side) | (block_of(source) == second), factor * values, values)


def level_of(rng, dims, split, least, high):
    loudness = 1.0
    for position, shards_of in split:
        steps = jax.random.uniform(jax.random.fold_in(jax.random.fold_in(rng, 6), position), (shards_of,), jnp.float32, least / len(split), high / len(split))
        loudness = loudness * jnp.repeat(jnp.exp(steps), dims[position] // shards_of).reshape((-1,) + (1,) * (len(dims) - 1 - position))
    return loudness


def shared_out(stream_key, own, number, rows, number_of, top, reach, skew):
    order = jax.random.permutation(stream_key, number_of)
    heavy_load, common = load_shares(number_of, rows * top, reach, skew, True), load_shares(number_of, rows * top, reach, skew, False)
    places = jnp.arange(number_of)

    def named(lengths, rotation):
        used = int((lengths > 0).sum())
        fixed = max(1, used // 4)
        shifted = fixed + (places - fixed + rotation * (used - fixed)) % max(1, number_of - fixed)
        return jnp.zeros((number_of,), jnp.int32).at[order[jnp.where(places < fixed, places, shifted)]].set(jnp.asarray(lengths, jnp.int32))

    lengths = jnp.where(number % 4 == 0, named(heavy_load, number // 4), named(common, number - number // 4 - 1))
    mixed = jax.random.permutation(jax.random.fold_in(own, 3), number_of)
    donor, receiver = mixed[0:number_of // 2 * 2:2], mixed[1:number_of // 2 * 2:2]
    room = jnp.minimum(lengths[donor] - 1, reach - lengths[receiver]) // 2
    room = jnp.where((donor == order[0]) | (receiver == order[0]) | (lengths[receiver] == 0), 0, jnp.maximum(room, 0))
    shifted = jax.random.randint(jax.random.fold_in(own, 4), (number_of // 2,), 0, 1 << 20) % (room + 1)
    lengths = lengths.at[donor].add(-shifted).at[receiver].add(shifted)
    members = jnp.searchsorted(jnp.cumsum(lengths), jnp.arange(rows * top), side="right").astype(jnp.int32)
    grid = members.reshape(top, rows).T
    grid = grid[jax.random.permutation(jax.random.fold_in(own, 1), rows)]
    rotation = jax.random.randint(jax.random.fold_in(own, 2), (rows, 1), 0, top)
    return jnp.take_along_axis(grid, (jnp.arange(top)[None, :] + rotation) % top, axis=1)


def load_shares(amount, total, reach, lean, full):
    weights = [(1 << 20) // math.isqrt(standing ** lean) + 1 for standing in range(1, amount + 1)]
    largest = reach if full else min(reach, max(-(-total // amount), total * weights[0] // sum(weights)))
    least = 1 if total - largest >= amount - 1 else 0
    holding, surplus = [largest] + [least] * (amount - 1), total - largest - least * (amount - 1)
    while surplus > 0:
        free = [i for i in range(1, amount) if holding[i] < largest] or [i for i in range(1, amount) if holding[i] < reach]
        mass, remaining = sum([weights[i] for i in free]), surplus
        for i in free:
            addition = min(reach - holding[i], max(1, remaining * weights[i] // mass), surplus)
            holding[i] = holding[i] + addition
            surplus = surplus - addition
    return np.array(holding)


def normal_values(key, extent, deviation, reach, cuts=(), kind=jnp.bfloat16):
    factor_of = level_of(key, extent, cuts, -0.22, 0.18) if cuts else 1.0
    entries = jax.random.normal(key, extent, jnp.float32) * deviation * factor_of
    return jnp.minimum(jnp.maximum(entries, -reach), reach).astype(kind)


def bell_draw_with(own_key, extent, width, limit, shards, heavy, held_as=jnp.bfloat16):
    values = width * jax.random.normal(own_key, extent, jnp.float32)
    if shards:
        values = values * level_of(own_key, extent, shards, -0.22, 0.18)
    return jnp.clip(spiked(values, jax.random.fold_in(own_key, 3), *heavy), -limit, limit).astype(held_as)


def setup_inputs(seed: int = 0) -> dict:
    arg_keys = jax.random.split(jax.random.key(seed), 8)
    words = bell_draw_with(arg_keys[0], (PAGES, PAGE_WORD_SLOTS, D), 1.0, 6.0, ((0, 32), (1, 8)), (0, 2, 32, 2.75))
    patches = normal_values(arg_keys[1], (PAGES, P_SIZE, D), 1.0, 6.0, ((0, 32), (1, 8)))
    proj = normal_values(arg_keys[2], (D, D), D ** -0.5, 0.1875, ((0, 32),))
    routes_keys = jax.random.split(jax.random.fold_in(arg_keys[3], 1), PAGES * PAGE_WORD_SLOTS // W_DEV)
    routes_turns = jax.random.permutation(jax.random.fold_in(arg_keys[3], 3), PAGES * PAGE_WORD_SLOTS // W_DEV)
    routes = jax.vmap(lambda own, number: shared_out(jax.random.fold_in(arg_keys[3], 2), own, number, W_DEV, N_SEQ, 1, CAP, 2))(routes_keys, routes_turns).reshape((PAGES, PAGE_WORD_SLOTS, 1))
    targets = with_ends(jax.random.randint(arg_keys[4], (PAGES, PAGE_WORD_SLOTS), 0, PPS), jax.random.fold_in(arg_keys[4], 1), 0, PPS - 1).astype(jnp.int32)
    counts = draw_counts(jax.random.fold_in(arg_keys[7], 71), 0)
    flags = with_ends((jax.random.randint(arg_keys[6], (PAGES, WB, PB), 0, 4) < 1).astype(jnp.int32), jax.random.fold_in(arg_keys[6], 1), 0, 1)
    return {"words": words, "patches": patches, "proj": proj, "routes": routes, "targets": targets, "counts": counts, "flags": flags}


def reference(words, patches, proj, routes, targets, counts, flags):
    scale = 2.0 / math.sqrt(D)
    capacity_limit = 2 * PAGE_WORD_SLOTS // (N_SEQ * N_SEQ)
    wdev = PAGE_WORD_SLOTS // N_SEQ
    pps = P_SIZE // N_SEQ
    bps = pps // MARGIN_BLOCK_SIZE
    nblk = PAGE_WORD_SLOTS // MARGIN_BLOCK_SIZE

    def page(grad, inputs):
        feats, patch, route, target, routed_count, flag = inputs
        query = jnp.dot(feats, proj, preferred_element_type=jnp.float32).astype(jnp.bfloat16)
        destination_slot = route[:, 0]
        home = jnp.arange(PAGE_WORD_SLOTS, dtype=jnp.int32) // wdev
        onehot = (destination_slot[:, None] == jnp.arange(N_SEQ, dtype=jnp.int32)[None, :]).astype(jnp.int32)
        onehot = onehot.reshape(N_SEQ, wdev, N_SEQ)
        rank = jnp.cumsum(onehot, axis=1) - onehot
        slot = lax.optimization_barrier(jnp.sum(rank * onehot, axis=2)).reshape(PAGE_WORD_SLOTS)
        column_offset = home * capacity_limit + slot
        qbuf = jnp.zeros((N_SEQ, N_SEQ * capacity_limit, D), jnp.bfloat16).at[destination_slot, column_offset].set(query)
        tbuf = jnp.zeros((N_SEQ, N_SEQ * capacity_limit), jnp.int32).at[destination_slot, column_offset].set(target)
        index_buffer = jnp.full((N_SEQ, N_SEQ * capacity_limit), -1, jnp.int32).at[destination_slot, column_offset].set(jnp.arange(PAGE_WORD_SLOTS, dtype=jnp.int32))
        patch_s = patch.reshape(N_SEQ, pps, D)
        scores = jnp.einsum('sud,skd->suk', qbuf.astype(jnp.float32), patch_s.astype(jnp.float32)) * scale
        table = flag.reshape(nblk, N_SEQ, bps).transpose(1, 0, 2)
        word_block = jnp.maximum(index_buffer, 0) // MARGIN_BLOCK_SIZE
        hit = jnp.take_along_axis(table, jnp.broadcast_to(word_block[:, :, None], (N_SEQ, N_SEQ * capacity_limit, bps)), axis=1)
        allowed = (hit > 0) | ((tbuf // MARGIN_BLOCK_SIZE)[:, :, None] == jnp.arange(bps, dtype=jnp.int32)[None, None, :])
        mask = jnp.broadcast_to(allowed[..., None], allowed.shape + (MARGIN_BLOCK_SIZE,)).reshape(scores.shape)
        expo = jnp.where(mask, jnp.exp(scores), jnp.float32(0.0))
        total = lax.optimization_barrier(jnp.sum(expo, axis=-1))
        is_target = jnp.arange(pps, dtype=jnp.int32)[None, None, :] == tbuf[:, :, None]
        target_score = lax.optimization_barrier(jnp.sum(jnp.where(is_target, scores, jnp.float32(0.0)), axis=-1))
        valid_mask = (index_buffer >= 0) & (index_buffer < routed_count)
        loss = jnp.where(valid_mask, jnp.log(total) - target_score, jnp.float32(0.0))
        coef = jnp.where(valid_mask, jnp.float32(64.0) / routed_count.astype(jnp.float32), jnp.float32(0.0))
        dscore = (coef[..., None] * (expo / total[..., None] - is_target.astype(jnp.float32))).astype(jnp.bfloat16)
        dquery = (jnp.einsum('suk,skd->sud', dscore.astype(jnp.float32), patch_s.astype(jnp.float32)) * scale).astype(jnp.bfloat16)
        dq_words = dquery[destination_slot, column_offset]
        loss_words = loss[destination_slot, column_offset]
        grad = grad + jnp.dot(feats.T, dq_words, preferred_element_type=jnp.float32)
        return (grad, loss_words)
    grad, losses = lax.scan(page, jnp.zeros((D, D), jnp.float32), (words, patches, routes, targets, counts, flags))
    return (losses, grad)
```

```python
import functools
import math

import jax
import jax.numpy as jnp
from jax import lax
from jax.experimental import pallas as pl
from jax.experimental.pallas import tpu as pltpu
from jax.sharding import PartitionSpec as P

MESH = pl.DeviceIdType.MESH
NX, NY, NZ = 4, 4, 8
NSEQ = 8
BLOCK = 64
F32, BF16, I32 = jnp.float32, jnp.bfloat16, jnp.int32
PEERS = ((2, 0), (2, 1), (1, 0), (1, 1), (3, 0), (3, 1), (0, 1))
DXS = (2, 1, 3)
DYS = (2, 1, 3)


def dot(a, b):
    return lax.dot_general(a, b, (((1,), (0,)), ((), ())), preferred_element_type=F32)


def dot_nt(a, b):
    return lax.dot_general(a, b, (((1,), (1,)), ((), ())), preferred_element_type=F32)


def dot_tn(a, b):
    return lax.dot_general(a, b, (((0,), (0,)), ((), ())), preferred_element_type=F32)


def iota(shape, dim):
    return lax.broadcasted_iota(I32, shape, dim)


def kernel(
    words_h, patches_h, proj_h, routes_r, targets_r, counts_s, flags_r,
    loss_o, grad_o,
    words_v, patches_v, proj_v, send_v, recv_v, meta_v, code_v, val_v,
    grad_v, dq_v, q_v, loss_s, loss_r,
    pair_s, pair_r, sum_v, a_s, a_r, b_s, b_r, a2_s, a2_r, b2_s, b2_r, z3_f, z3_s, z3_r,
    loc_sem, disp_ss, disp_rs, meta_ss, meta_rs, agz_ss, agz_rs, agx_ss, agx_rs, sib_ss, sib_rs,
    loss_ss, loss_rs, pair_ss, pair_rs, a_ss, a_rs, b_ss, b_rs, a2_ss, a2_rs, b2_ss, b2_rs, z3_ss, z3_rs,
):
    pages, wdev, width = words_v.shape
    ppsz = patches_v.shape[1]
    cap = 2 * wdev // NSEQ
    scale = 2.0 / math.sqrt(width)
    d = lax.axis_index("dp")
    s = lax.axis_index("seq")
    x, z = d // NZ, d % NZ
    y, c = s // 2, s % 2

    def seq_of(dy, dc):
        return ((y + dy) % NY) * 2 + (c + dc) % 2

    def to_seq(dy, dc):
        return {"dp": d, "seq": seq_of(dy, dc)}

    def to_x(dx):
        return {"dp": ((x + dx) % NX) * NZ + z, "seq": s}

    def to_z(dz):
        return {"dp": x * NZ + (z + dz) % NZ, "seq": s}

    def remote(src, dst, ss, rs, dev):
        return pltpu.make_async_remote_copy(
            src_ref=src, dst_ref=dst, send_sem=ss, recv_sem=rs, device_id=dev, device_id_type=MESH
        )

    sent = []

    def go(cp):
        cp.start()
        sent.append(cp)
        return cp

    rows = proj_h.shape[0]
    loads = [
        pltpu.make_async_copy(words_h.at[p], words_v.at[p], loc_sem.at[p]) for p in range(pages)
    ]
    for k in range(2):
        cols = pl.ds(pl.multiple_of((2 * c + k) * 256, 256), 256)
        loads.append(
            pltpu.make_async_copy(
                proj_h.at[:, cols],
                proj_v.at[2 * c + k, pl.ds(pl.multiple_of(d * rows, rows), rows)],
                loc_sem.at[pages + k],
            )
        )
    loads.append(pltpu.make_async_copy(patches_h, patches_v, loc_sem.at[pages + 2]))
    for cp in loads:
        cp.start()

    barrier = pltpu.get_barrier_semaphore()
    greet = [to_seq(*t) for t in PEERS] + [to_x(i) for i in DXS] + [to_z(i) for i in range(1, NZ)]
    for dev in greet:
        pl.semaphore_signal(barrier, inc=1, device_id=dev, device_id_type=MESH)

    routes = routes_r[...]
    meta_v[s, 0:pages, :] = routes
    meta_v[s, pages : 2 * pages, :] = targets_r[...]
    upper = (iota((wdev, wdev), 0) < iota((wdev, wdev), 1)).astype(BF16)
    for p in range(pages):
        route = jnp.broadcast_to(routes[p : p + 1, :], (NSEQ, wdev))
        hot = route == iota((NSEQ, wdev), 0)
        rank = dot(hot.astype(BF16), upper)
        slot = jnp.sum(jnp.where(hot, rank, 0.0), axis=0, keepdims=True).astype(I32)
        code = routes[p : p + 1, :] * cap + slot
        pick = (jnp.broadcast_to(code, (NSEQ * cap, wdev)) == iota((NSEQ * cap, wdev), 0)).astype(F32).astype(BF16)
        loads[p].wait()
        buf = dot(pick, words_v[p]).astype(BF16)
        send_v[p] = buf.reshape(NSEQ, cap, width)
        recv_v[p, s] = send_v[p, s]

    pl.semaphore_wait(barrier, len(greet))

    def dispatch(p, i):
        dy, dc = PEERS[i]
        return remote(
            send_v.at[p, seq_of(dy, dc)], recv_v.at[p, s], disp_ss.at[p, i], disp_rs.at[p, i], to_seq(dy, dc)
        )

    def send_page(p):
        for i in range(len(PEERS)):
            go(dispatch(p, i))

    def ag_z(k, i):
        own = proj_v.at[2 * c + k, pl.ds(pl.multiple_of(d * rows, rows), rows)]
        return remote(own, own, agz_ss.at[k, i - 1], agz_rs.at[k, i - 1], to_z(i))

    xrows = width // NX

    def pblock(k, xb, lo, n):
        return proj_v.at[2 * c + k, pl.ds(pl.multiple_of(xb * xrows + lo, 128), n)]

    def ag_x(k, hop):
        half = xrows // 2
        ref, dx = (
            (pblock(k, x, 0, xrows), 1),
            (pblock(k, x, 0, xrows), 3),
            (pblock(k, (x + 3) % NX, 0, half), 1),
            (pblock(k, (x + 1) % NX, half, half), 3),
        )[hop]
        return remote(ref, ref, agx_ss.at[k, hop], agx_rs.at[k, hop], to_x(dx))

    def ag_sib(k, dx):
        ref = pblock(k, (x + dx) % NX, 0, xrows)
        return remote(ref, ref, sib_ss.at[k, dx], sib_rs.at[k, dx], to_seq(0, 1))

    send_page(0)
    for k in range(2):
        loads[pages + k].wait()
        for i in range(1, NZ):
            go(ag_z(k, i))
    meta_cp = []
    for i, (dy, dc) in enumerate(PEERS):
        meta_cp.append(go(remote(meta_v.at[s], meta_v.at[s], meta_ss.at[i], meta_rs.at[i], to_seq(dy, dc))))
    for p in range(1, pages):
        send_page(p)

    grad_v[...] = jnp.zeros_like(grad_v)

    for k in range(2):
        for i in range(1, NZ):
            ag_z(k, i).wait_recv()
        go(ag_x(k, 0))
        go(ag_x(k, 1))
        go(ag_sib(k, 0))

    for cp in meta_cp:
        cp.wait_recv()
    for h in range(NSEQ):
        here = meta_v[h, 0:pages, :] == s
        rank = dot(here.astype(F32).astype(BF16), upper)
        code_v[h] = jnp.where(here, rank.astype(I32), -1)
        val_v[h] = (meta_v[h, pages : 2 * pages, :] + iota((pages, wdev), 1) * ppsz + 1).astype(F32)

    for k in range(2):
        ag_x(k, 0).wait_recv()
        ag_x(k, 1).wait_recv()
        go(ag_x(k, 2))
        go(ag_x(k, 3))
        go(ag_sib(k, 1))
        go(ag_sib(k, 3))
    for k in range(2):
        ag_x(k, 2).wait_recv()
        ag_x(k, 3).wait_recv()
        go(ag_sib(k, 2))
    loads[pages + 2].wait()
    for k in range(2):
        for dx in range(NX):
            ag_sib(k, dx).wait_recv()

    n_slots = NSEQ * cap
    spread = (iota((4 * NSEQ, ppsz), 0) == s * (ppsz // BLOCK) + iota((4 * NSEQ, ppsz), 1) // BLOCK).astype(F32).astype(BF16)
    home = iota((n_slots, 1), 0) // cap
    cand = iota((n_slots, ppsz), 1)

    def front(p):
        for i in range(len(PEERS)):
            dispatch(p, i).wait_recv()
        got = recv_v[p].reshape(n_slots, width)
        for k in range(4):
            q_v[:, k * 256 : (k + 1) * 256] = dot(got, proj_v[k]).astype(BF16)
        scores = dot_nt(q_v[...], patches_v[p]) * scale
        own = [
            jnp.broadcast_to(code_v[h, pl.ds(p, 1), :], (cap, wdev)) == iota((cap, wdev), 0) for h in range(NSEQ)
        ]
        val = jnp.concatenate(
            [
                jnp.sum(jnp.where(own[h], jnp.broadcast_to(val_v[h, pl.ds(p, 1), :], (cap, wdev)), 0.0), axis=1, keepdims=True)
                for h in range(NSEQ)
            ],
            axis=0,
        ).astype(I32)
        packed = jnp.maximum(val - 1, 0)
        tgt = packed % ppsz
        word = home * wdev + packed // ppsz
        hit = dot(
            (word // BLOCK == iota((n_slots, 2 * NSEQ), 1)).astype(F32).astype(BF16),
            dot(flags_r[p].astype(F32).astype(BF16), spread).astype(BF16),
        )
        allowed = (hit > 0.0) | (tgt // BLOCK == cand // BLOCK)
        expo = jnp.where(allowed, jnp.exp(scores), 0.0)
        total = jnp.sum(expo, axis=1, keepdims=True)
        is_t = cand == tgt
        t_score = jnp.sum(jnp.where(is_t, scores, 0.0), axis=1, keepdims=True)
        count = counts_s[p]
        valid = (val > 0) & (word < count)
        loss = jnp.where(valid, jnp.log(total) - t_score, 0.0)
        coef = jnp.where(valid, 64.0 / jnp.full((n_slots, 1), count, I32).astype(F32), 0.0)
        dscore = (coef * (expo * (1.0 / total) - jnp.where(is_t, 1.0, 0.0))).astype(BF16)
        dq = (dot(dscore, patches_v[p]) * scale).astype(BF16)
        for j in range(NSEQ):
            at = ((j + c) % 2) * (width // 2) + (j // 2) * 128
            dq_v[:, pl.ds(pl.multiple_of(at, 128), 128)] = dq[:, j * 128 : (j + 1) * 128]
        for h in range(NSEQ):
            loss_s[h, pl.ds(p, 1), :] = jnp.sum(
                jnp.where(own[h], jnp.broadcast_to(loss[h * cap : (h + 1) * cap], (cap, wdev)), 0.0),
                axis=0,
                keepdims=True,
            )

    def page(p, carry):
        front(p)
        for r in range(4):
            grad_v[r * 256 : (r + 1) * 256, :] += dot_tn(
                recv_v[p, :, :, r * 256 : (r + 1) * 256].reshape(n_slots, 256), dq_v[...]
            )
        return carry

    lax.fori_loop(0, pages - 1, page, 0)
    last = pages - 1
    front(last)

    loss_cp = []
    for i, (dy, dc) in enumerate(PEERS):
        loss_cp.append(
            go(remote(loss_s.at[seq_of(dy, dc)], loss_r.at[i], loss_ss.at[i], loss_rs.at[i], to_seq(dy, dc)))
        )

    half = width // 2
    order = [(x + i) % NX for i in DXS] + [x]
    pair_cp = []
    for i, xb in enumerate(order):
        at = pl.ds(pl.multiple_of(xb * 256, 256), 256)
        g = grad_v[at, :] + dot_tn(recv_v[last, :, :, at].reshape(n_slots, 256), dq_v[...])
        pair_s[i] = g[:, half:].astype(BF16)
        pair_cp.append(go(remote(pair_s.at[i], pair_r.at[i], pair_ss.at[i], pair_rs.at[i], to_seq(0, 1))))
        sum_v[i] = g[:, :half]

    def ycols(dy):
        return pl.ds(pl.multiple_of(((y + dy) % NY) * 128, 128), 128)

    a_cp, b_cp = [], []
    for i in range(NX):
        pair_cp[i].wait_recv()
        t = (sum_v[i] + pair_r[i].astype(F32)).reshape(NZ, 2, 16, half)
        sum_v[i] = t.reshape(256, half)
        if i < 3:
            a_s[i] = t[:, 0].astype(BF16)
            a_cp.append(go(remote(a_s.at[i], a_r.at[i], a_ss.at[i], a_rs.at[i], to_x(DXS[i]))))
        for j in range(3):
            b_s[j, i] = sum_v[i, :, ycols(DYS[j])].reshape(NZ, 2, 16, 128)[:, 1].astype(BF16)
            b_cp.append(go(remote(b_s.at[j, i], b_r.at[j, i], b_ss.at[j, i], b_rs.at[j, i], to_seq(DYS[j], 0))))
    for cp in a_cp:
        cp.wait_recv()
    t = sum_v[3].reshape(NZ, 2, 16, half)
    acc = t[:, 0]
    for i in range(3):
        acc = acc + a_r[i].astype(F32)
    sum_v[3] = jnp.concatenate([acc[:, None], t[:, 1:2]], axis=1).reshape(256, half)
    a2_cp, b2_cp = [], []
    for j in range(3):
        a2_s[j] = sum_v[3, :, ycols(DYS[j])].reshape(NZ, 2, 16, 128)[:, 0].astype(BF16)
        a2_cp.append(go(remote(a2_s.at[j], a2_r.at[j], a2_ss.at[j], a2_rs.at[j], to_seq(DYS[j], 0))))
    for cp in b_cp:
        cp.wait_recv()
    for i in range(NX):
        acc = sum_v[i, :, ycols(0)].reshape(NZ, 2, 16, 128)[:, 1]
        for j in range(3):
            acc = acc + b_r[j, i].astype(F32)
        if i < 3:
            b2_s[i] = acc.astype(BF16)
            b2_cp.append(go(remote(b2_s.at[i], b2_r.at[i], b2_ss.at[i], b2_rs.at[i], to_x(DXS[i]))))
    acc_b = acc
    acc_a = sum_v[3, :, ycols(0)].reshape(NZ, 2, 16, 128)[:, 0]
    for cp in a2_cp + b2_cp:
        cp.wait_recv()
    for j in range(3):
        acc_a = acc_a + a2_r[j].astype(F32)
        acc_b = acc_b + b2_r[j].astype(F32)
    z3_f[:, 0:16, :] = acc_a
    z3_f[:, 16:32, :] = acc_b
    z3_s[...] = z3_f[...].astype(BF16)
    z3_cp = []
    for i in range(1, NZ):
        z3_cp.append(go(remote(z3_s.at[(z + i) % NZ], z3_r.at[i - 1], z3_ss.at[i - 1], z3_rs.at[i - 1], to_z(i))))
    for cp in loss_cp:
        cp.wait_recv()
    loss_o[...] = loss_s[s] + jnp.sum(loss_r[...], axis=0)
    for cp in z3_cp:
        cp.wait_recv()
    grad_o[...] = z3_f[z] + jnp.sum(z3_r[...].astype(F32), axis=0)
    for cp in sent:
        cp.wait_send()


def local(words, patches, proj, routes, targets, counts, flags):
    pages, wdev, width = words.shape
    ppsz = patches.shape[1]
    cap = 2 * wdev // NSEQ
    half = width // 2
    vm = pltpu.VMEM
    dma = pltpu.SemaphoreType.DMA
    any_ = pl.BlockSpec(memory_space=pl.ANY)
    vmem = pl.BlockSpec(memory_space=pltpu.VMEM)
    pairs = [(pages, 7), (7,), (2, 7), (2, 4), (2, 4), (7,), (4,), (3,), (3, 4), (3,), (3,), (7,)]
    loss, grad = pl.pallas_call(
        kernel,
        out_shape=(
            jax.ShapeDtypeStruct((pages, wdev), F32),
            jax.ShapeDtypeStruct((width // (NX * NZ), width // NSEQ), F32),
        ),
        in_specs=[any_, any_, any_, vmem, vmem, pl.BlockSpec(memory_space=pltpu.SMEM), vmem],
        out_specs=(vmem, vmem),
        scratch_shapes=[
            vm((pages, wdev, width), BF16),
            vm((pages, ppsz, width), BF16),
            vm((4, width, 256), BF16),
            vm((pages, NSEQ, cap, width), BF16),
            vm((pages, NSEQ, cap, width), BF16),
            vm((NSEQ, 2 * pages, wdev), I32),
            vm((NSEQ, pages, wdev), I32),
            vm((NSEQ, pages, wdev), F32),
            vm((width, width), F32),
            vm((NSEQ * cap, width), BF16),
            vm((NSEQ * cap, width), BF16),
            vm((NSEQ, pages, wdev), F32),
            vm((7, pages, wdev), F32),
            vm((NX, 256, half), BF16),
            vm((NX, 256, half), BF16),
            vm((NX, 256, half), F32),
            vm((3, NZ, 16, half), BF16),
            vm((3, NZ, 16, half), BF16),
            vm((3, NX, NZ, 16, 128), BF16),
            vm((3, NX, NZ, 16, 128), BF16),
            vm((3, NZ, 16, 128), BF16),
            vm((3, NZ, 16, 128), BF16),
            vm((3, NZ, 16, 128), BF16),
            vm((3, NZ, 16, 128), BF16),
            vm((NZ, 32, 128), F32),
            vm((NZ, 32, 128), BF16),
            vm((7, 32, 128), BF16),
            dma((pages + 3,)),
        ]
        + [dma(shape) for shape in pairs for _ in range(2)],
        compiler_params=pltpu.CompilerParams(collective_id=1, has_side_effects=True, vmem_limit_bytes=56 << 20),
        name="grounding",
    )(words, patches, proj, routes.reshape(pages, wdev), targets, counts, flags)
    return loss, grad


def solution(mesh):
    in_specs = (
        P("dp", "seq", None),
        P("dp", "seq", None),
        P("dp", None),
        P("dp", "seq", None),
        P("dp", "seq"),
        P("dp"),
        P("dp", None, None),
    )
    out_specs = (P("dp", "seq"), P("dp", "seq"))
    return jax.shard_map(local, mesh=mesh, in_specs=in_specs, out_specs=out_specs, check_vma=False)
```

```python
import functools
import math

import jax
import jax.numpy as jnp
from jax import lax
from jax.experimental import pallas as pl
from jax.experimental.pallas import tpu as pltpu
from jax.sharding import PartitionSpec as P

MESH = pl.DeviceIdType.MESH
NX, NY, NZ = 4, 4, 8
NSEQ = 8
BLOCK = 64
F32, BF16, I32 = jnp.float32, jnp.bfloat16, jnp.int32
PEERS = ((2, 0), (2, 1), (1, 0), (1, 1), (3, 0), (3, 1), (0, 1))
DXS = (2, 1, 3)
DYS = (2, 1, 3)
ZORDER = (4, 3, 5, 2, 6, 1, 7)


def dot(a, b):
    return lax.dot_general(a, b, (((1,), (0,)), ((), ())), preferred_element_type=F32)


def dot_nt(a, b):
    return lax.dot_general(a, b, (((1,), (1,)), ((), ())), preferred_element_type=F32)


def dot_tn(a, b):
    return lax.dot_general(a, b, (((0,), (0,)), ((), ())), preferred_element_type=F32)


def iota(shape, dim):
    return lax.broadcasted_iota(I32, shape, dim)


def kernel(
    words_h, patches_h, proj_h, routes_h, targets_h, counts_h, flags_h,
    loss_o, grad_o,
    routes_r, targets_r, counts_s, flags_r, words_v, patches_v, proj_v, send_v, recv_v, meta_v, code_v, val_v,
    grad_v, mask_v, tgt_v, coef_v, loss_v, dq_v, q_v, loss_s, loss_r,
    pair_s, pair_r, sum_v, a_s, a_r, ar_r, a_f, b_s, b_r, br_r, a2_s, a2_r, b2_s, b2_r, z3_f, z3_s, z3_r,
    loc_sem, disp_ss, disp_rs, meta_ss, meta_rs, aga_ss, aga_rs, agb_ss, agb_rs, sib_ss, sib_rs,
    loss_ss, loss_rs, pair_ss, pair_rs, a_ss, a_rs, ar_ss, ar_rs, b_ss, b_rs, br_ss, br_rs, a2_ss, a2_rs, b2_ss, b2_rs, z3_ss, z3_rs,
):
    pages, wdev, width = words_v.shape
    ppsz = patches_v.shape[1]
    cap = 2 * wdev // NSEQ
    scale = 2.0 / math.sqrt(width)
    d = lax.axis_index("dp")
    s = lax.axis_index("seq")
    x, z = d // NZ, d % NZ
    y, c = s // 2, s % 2

    def seq_of(dy, dc):
        return ((y + dy) % NY) * 2 + (c + dc) % 2

    def to_seq(dy, dc):
        return {"dp": d, "seq": seq_of(dy, dc)}

    def to_x(dx):
        return {"dp": ((x + dx) % NX) * NZ + z, "seq": s}

    def to_z(dz):
        return {"dp": x * NZ + (z + dz) % NZ, "seq": s}

    def remote(src, dst, ss, rs, dev):
        return pltpu.make_async_remote_copy(
            src_ref=src, dst_ref=dst, send_sem=ss, recv_sem=rs, device_id=dev, device_id_type=MESH
        )

    sent = []

    def go(cp):
        cp.start()
        sent.append(cp)
        return cp

    barrier = pltpu.get_barrier_semaphore()
    greet = [to_seq(*t) for t in PEERS] + [to_x(i) for i in DXS] + [to_z(i) for i in range(1, NZ)]
    for dev in greet:
        pl.semaphore_signal(barrier, inc=1, device_id=dev, device_id_type=MESH)

    rows = proj_h.shape[0]
    loads = [
        pltpu.make_async_copy(words_h.at[p], words_v.at[p], loc_sem.at[p]) for p in range(pages)
    ]
    for k in range(2):
        cols = pl.ds(pl.multiple_of((2 * c + k) * 256, 256), 256)
        loads.append(
            pltpu.make_async_copy(
                proj_h.at[:, cols],
                proj_v.at[2 * c + k, x, pl.ds(pl.multiple_of(z * rows, rows), rows)],
                loc_sem.at[pages + k],
            )
        )
    loads.append(pltpu.make_async_copy(patches_h, patches_v, loc_sem.at[pages + 2]))
    small = [
        pltpu.make_async_copy(src, dst, loc_sem.at[pages + 3 + i])
        for i, (src, dst) in enumerate(
            ((routes_h, routes_r), (targets_h, targets_r), (counts_h, counts_s), (flags_h, flags_r))
        )
    ]
    for cp in small + loads:
        cp.start()
    for cp in small:
        cp.wait()

    routes = routes_r[...]
    meta_v[s, 0:pages, :] = routes
    meta_v[s, pages : 2 * pages, :] = targets_r[...]
    upper = (iota((wdev, wdev), 0) < iota((wdev, wdev), 1)).astype(BF16)
    lanes = jnp.concatenate([jnp.broadcast_to(routes[p : p + 1, :], (NSEQ, wdev)) for p in range(pages)], axis=0)
    hot = lanes == iota((pages * NSEQ, wdev), 0) % NSEQ
    rank = jnp.where(hot, dot(hot.astype(F32).astype(BF16), upper), 0.0)

    def build(p):
        slot = jnp.sum(rank[p * NSEQ : (p + 1) * NSEQ], axis=0, keepdims=True).astype(I32)
        code = routes[p : p + 1, :] * cap + slot
        pick = (jnp.broadcast_to(code, (NSEQ * cap, wdev)) == iota((NSEQ * cap, wdev), 0)).astype(F32).astype(BF16)
        loads[p].wait()
        send_v[p] = dot(pick, words_v[p]).astype(BF16).reshape(NSEQ, cap, width)

    build(0)
    pl.semaphore_wait(barrier, len(greet))

    def dispatch(p, i):
        dy, dc = PEERS[i]
        return remote(
            send_v.at[p, seq_of(dy, dc)], recv_v.at[p, s], disp_ss.at[p, i], disp_rs.at[p, i], to_seq(dy, dc)
        )

    def send_page(p):
        for i in range(len(PEERS)):
            go(dispatch(p, i))

    def zrows(zb):
        return pl.ds(pl.multiple_of(zb * rows, rows), rows)

    half = rows * NZ // 2

    def ag_a(hop, i=0):
        if hop == 0:
            ref, dev = proj_v.at[2 * c, x, zrows(z)], to_z(i)
        elif hop == 1:
            ref, dev = proj_v.at[2 * c, x], to_x((1, 3)[i])
        else:
            ref, dev = proj_v.at[2 * c, (x + (3, 1)[i]) % NX, i * half : (i + 1) * half], to_x((1, 3)[i])
        at = i - 1 if hop == 0 else NZ - 1 + 2 * (hop - 1) + i
        return remote(ref, ref, aga_ss.at[at], aga_rs.at[at], dev)

    def ag_b(hop, i):
        if hop == 0:
            ref, dev = proj_v.at[2 * c + 1, x, zrows(z)], to_x(DXS[i])
        else:
            ref, dev = proj_v.at[2 * c + 1, :, zrows(z)], to_z(i)
        at = i if hop == 0 else 2 + i
        return remote(ref, ref, agb_ss.at[at], agb_rs.at[at], dev)

    def sib_a(dx):
        ref = proj_v.at[2 * c, (x + dx) % NX]
        return remote(ref, ref, sib_ss.at[dx], sib_rs.at[dx], to_seq(0, 1))

    def sib_b(i):
        ref = proj_v.at[2 * c + 1, :, zrows((z + i) % NZ)]
        return remote(ref, ref, sib_ss.at[NX + i], sib_rs.at[NX + i], to_seq(0, 1))

    meta_cp = []
    for i, (dy, dc) in enumerate(PEERS):
        meta_cp.append(go(remote(meta_v.at[s], meta_v.at[s], meta_ss.at[i], meta_rs.at[i], to_seq(dy, dc))))
    send_page(0)
    for i in range(2):
        loads[pages + i].wait()
    for i in range(3):
        go(ag_b(0, i))
    for i in range(1, NZ):
        go(ag_a(0, i))
    build(1)
    send_page(1)
    build(2)
    send_page(2)
    for i in range(3):
        ag_b(0, i).wait_recv()
    for i in ZORDER:
        go(ag_b(1, i))
    go(sib_b(0))
    build(3)
    send_page(3)
    for p in range(pages):
        recv_v[p, s] = send_v[p, s]
    for i in range(1, NZ):
        ag_a(0, i).wait_recv()
    for i in range(2):
        go(ag_a(1, i))
    go(sib_a(0))

    for cp in meta_cp:
        cp.wait_recv()
    for h in range(NSEQ):
        here = meta_v[h, 0:pages, :] == s
        rank = dot(here.astype(F32).astype(BF16), upper)
        code_v[h] = jnp.where(here, rank.astype(I32), -1)
        val_v[h] = (meta_v[h, pages : 2 * pages, :] + iota((pages, wdev), 1) * ppsz + 1).astype(F32)

    n_slots = NSEQ * cap
    spread = (iota((4 * NSEQ, ppsz), 0) == s * (ppsz // BLOCK) + iota((4 * NSEQ, ppsz), 1) // BLOCK).astype(F32).astype(BF16)
    home = iota((n_slots, 1), 0) // cap
    cand = iota((n_slots, ppsz), 1)

    def owned(p):
        return [
            jnp.broadcast_to(code_v[h, pl.ds(p, 1), :], (cap, wdev)) == iota((cap, wdev), 0) for h in range(NSEQ)
        ]

    def prepare(p):
        own = owned(p)
        val = jnp.concatenate(
            [
                jnp.sum(jnp.where(own[h], jnp.broadcast_to(val_v[h, pl.ds(p, 1), :], (cap, wdev)), 0.0), axis=1, keepdims=True)
                for h in range(NSEQ)
            ],
            axis=0,
        ).astype(I32)
        packed = jnp.maximum(val - 1, 0)
        tgt = packed % ppsz
        word = home * wdev + packed // ppsz
        hit = dot(
            (word // BLOCK == iota((n_slots, 2 * NSEQ), 1)).astype(F32).astype(BF16),
            dot(flags_r[p].astype(F32).astype(BF16), spread).astype(BF16),
        )
        allowed = (hit > 0.0) | (tgt // BLOCK == cand // BLOCK)
        mask_v[p] = allowed.astype(F32).astype(BF16)
        tgt_v[p] = tgt
        count = counts_s[p]
        valid = (val > 0) & (word < count)
        coef_v[p] = jnp.where(valid, 64.0 / jnp.full((n_slots, 1), count, I32).astype(F32), 0.0)

    for p in range(2):
        prepare(p)
    for i in range(2):
        ag_a(1, i).wait_recv()
    for i in range(2):
        go(ag_a(2, i))
    go(sib_a(1))
    go(sib_a(3))
    for p in range(2, pages):
        prepare(p)
    for i in ZORDER:
        ag_b(1, i).wait_recv()
        go(sib_b(NZ - i))
    for i in range(2):
        ag_a(2, i).wait_recv()
    go(sib_a(2))
    loads[pages + 2].wait()
    for i in range(NZ):
        sib_b(i).wait_recv()
    for i in range(NX):
        sib_a(i).wait_recv()

    def front(p):
        for i in range(len(PEERS)):
            dispatch(p, i).wait_recv()
        got = recv_v[p].reshape(n_slots, width)
        for k in range(4):
            q_v[:, k * 256 : (k + 1) * 256] = dot(got, proj_v[k].reshape(width, 256)).astype(BF16)
        scores = dot_nt(q_v[...], patches_v[p]) * scale
        expo = jnp.where(mask_v[p].astype(F32) > 0.0, jnp.exp(scores), 0.0)
        total = jnp.sum(expo, axis=1, keepdims=True)
        is_t = cand == tgt_v[p]
        t_score = jnp.sum(jnp.where(is_t, scores, 0.0), axis=1, keepdims=True)
        coef = coef_v[p]
        loss_v[p] = jnp.where(coef > 0.0, jnp.log(total) - t_score, 0.0)
        dscore = (coef * (expo * (1.0 / total) - jnp.where(is_t, 1.0, 0.0))).astype(BF16)
        dq = (dot(dscore, patches_v[p]) * scale).astype(BF16)
        for j in range(NSEQ):
            at = ((j + c) % 2) * (width // 2) + (j // 2) * 128
            dq_v[p, :, pl.ds(pl.multiple_of(at, 128), 128)] = dq[:, j * 128 : (j + 1) * 128]

    def send_home(p):
        own, loss = owned(p), loss_v[p]
        for h in range(NSEQ):
            loss_s[h, pl.ds(p, 1), :] = jnp.sum(
                jnp.where(own[h], jnp.broadcast_to(loss[h * cap : (h + 1) * cap], (cap, wdev)), 0.0),
                axis=0,
                keepdims=True,
            )

    def page(p, carry):
        front(p)
        send_home(p)
        return carry

    last = pages - 1
    lax.fori_loop(0, last, page, 0)
    for r in range(4):
        grad_v[r * 256 : (r + 1) * 256, :] = dot_tn(
            recv_v[0:last, :, :, r * 256 : (r + 1) * 256].reshape(last * n_slots, 256),
            dq_v[0:last].reshape(last * n_slots, width),
        )
    front(last)

    n_early = len(sent)

    half = width // 2
    order = [(x + i) % NX for i in DXS] + [x]
    pair_cp = []
    for i, xb in enumerate(order):
        at = pl.ds(pl.multiple_of(xb * 256, 256), 256)
        g = grad_v[at, :] + dot_tn(recv_v[last, :, :, at].reshape(n_slots, 256), dq_v[last])
        pair_s[i] = g[:, half:].astype(BF16)
        pair_cp.append(go(remote(pair_s.at[i], pair_r.at[i], pair_ss.at[i], pair_rs.at[i], to_seq(0, 1))))
        sum_v[i] = g[:, :half]

    def ycols(dy):
        return pl.ds(pl.multiple_of(((y + dy) % NY) * 128, 128), 128)

    def part(i, which, cols=None):
        ref = sum_v[i] if cols is None else sum_v[i, :, cols]
        return ref.reshape(NZ, 2, 16, ref.shape[-1])[:, which]

    zh = NZ // 2
    halves = (slice(0, zh), slice(zh, NZ))
    step = (1, 3)
    ar_cp, ad_cp, br_cp, bd_cp = [None] * 2, [None] * 2, [], []
    for i in range(NX):
        pair_cp[i].wait_recv()
        sum_v[i] += pair_r[i].astype(F32)
        if i == 0:
            a_s[0] = part(0, 0).astype(BF16)
            for w in range(2):
                src = a_s.at[0, pl.ds(w * zh, zh)]
                ar_cp[w] = go(remote(src, ar_r.at[w], ar_ss.at[w], ar_rs.at[w], to_x(step[w])))
        elif i < 3:
            w = i - 1
            a_s[1 + w, halves[1 - w]] = part(i, 0)[halves[1 - w]].astype(BF16)
            at = pl.ds((1 - w) * zh, zh)
            ad_cp[w] = go(remote(a_s.at[1 + w, at], a_r.at[w, at], a_ss.at[w, 0], a_rs.at[w, 0], to_x(step[w])))
        far = part(i, 1, ycols(2)).astype(BF16)
        for w in range(2):
            b_s[w, 0, i] = far[halves[w]]
            b_s[w, 1, i] = part(i, 1, ycols(step[w]))[halves[1 - w]].astype(BF16)
            br_cp.append(go(remote(b_s.at[w, 0, i], br_r.at[w, i], br_ss.at[w, i], br_rs.at[w, i], to_seq(step[w], 0))))
            bd_cp.append(
                go(remote(b_s.at[w, 1, i], b_r.at[w, 0, i], b_ss.at[w, 0, i], b_rs.at[w, 0, i], to_seq(step[w], 0)))
            )
    am_cp, bm_cp = [], []
    for w in range(2):
        ar_cp[w].wait_recv()
        a_s[1 + w, halves[w]] = (part(1 + w, 0)[halves[w]] + ar_r[w].astype(F32)).astype(BF16)
        at = pl.ds(w * zh, zh)
        am_cp.append(go(remote(a_s.at[1 + w, at], a_r.at[w, at], a_ss.at[w, 1], a_rs.at[w, 1], to_x(step[w]))))
    for i in range(NX):
        for w in range(2):
            br_cp[2 * i + w].wait_recv()
            b_s[w, 2, i] = (part(i, 1, ycols(step[w]))[halves[w]] + br_r[w, i].astype(F32)).astype(BF16)
            bm_cp.append(
                go(remote(b_s.at[w, 2, i], b_r.at[w, 1, i], b_ss.at[w, 1, i], b_rs.at[w, 1, i], to_seq(step[w], 0)))
            )
    send_home(last)
    loss_cp = []
    for i, (dy, dc) in enumerate(PEERS):
        loss_cp.append(
            go(remote(loss_s.at[seq_of(dy, dc)], loss_r.at[i], loss_ss.at[i], loss_rs.at[i], to_seq(dy, dc)))
        )
    for cp in sent[:n_early]:
        cp.wait_send()
    for cp in ad_cp + am_cp:
        cp.wait_recv()
    a_f[...] = part(3, 0) + a_r[0].astype(F32) + a_r[1].astype(F32)
    a2_cp, b2_cp = [], []
    for j in range(3):
        a2_s[j] = a_f[:, :, ycols(DYS[j])].astype(BF16)
        a2_cp.append(go(remote(a2_s.at[j], a2_r.at[j], a2_ss.at[j], a2_rs.at[j], to_seq(DYS[j], 0))))
    for cp in bd_cp + bm_cp:
        cp.wait_recv()
    for i in range(NX):
        left = jnp.concatenate([b_r[0, 1, i], b_r[0, 0, i]], axis=0).astype(F32)
        right = jnp.concatenate([b_r[1, 0, i], b_r[1, 1, i]], axis=0).astype(F32)
        acc_b = part(i, 1, ycols(0)) + left + right
        if i < 3:
            b2_s[i] = acc_b.astype(BF16)
            b2_cp.append(go(remote(b2_s.at[i], b2_r.at[i], b2_ss.at[i], b2_rs.at[i], to_x(DXS[i]))))
    acc_a = a_f[:, :, ycols(0)]
    n_mid = len(sent)
    for cp in a2_cp + b2_cp:
        cp.wait_recv()
    for j in range(3):
        acc_a = acc_a + a2_r[j].astype(F32)
        acc_b = acc_b + b2_r[j].astype(F32)
    z3_f[:, 0:16, :] = acc_a
    z3_f[:, 16:32, :] = acc_b
    z3_s[...] = z3_f[...].astype(BF16)
    z3_cp = []
    for i in range(1, NZ):
        z3_cp.append(go(remote(z3_s.at[(z + i) % NZ], z3_r.at[i - 1], z3_ss.at[i - 1], z3_rs.at[i - 1], to_z(i))))
    for cp in loss_cp:
        cp.wait_recv()
    loss_o[...] = loss_s[s] + jnp.sum(loss_r[...], axis=0)
    for cp in sent[n_early:n_mid]:
        cp.wait_send()
    for cp in z3_cp:
        cp.wait_recv()
    grad_o[...] = z3_f[z] + jnp.sum(z3_r[...].astype(F32), axis=0)
    for cp in sent[n_mid:]:
        cp.wait_send()


def finish(loss_r, grad_r, loss_o, grad_o):
    loss_o[...] = loss_r[...]
    grad_o[...] = grad_r[...]


def local(words, patches, proj, routes, targets, counts, flags):
    pages, wdev, width = words.shape
    ppsz = patches.shape[1]
    cap = 2 * wdev // NSEQ
    half = width // 2
    vm = pltpu.VMEM
    dma = pltpu.SemaphoreType.DMA
    any_ = pl.BlockSpec(memory_space=pl.ANY)
    vmem = pl.BlockSpec(memory_space=pltpu.VMEM)
    pairs = [(pages, 7), (7,), (NZ + 3,), (NZ + 2,), (NX + NZ,), (7,), (4,), (2, 2), (2,), (2, 2, 4), (2, 4), (3,), (3,), (7,)]
    loss, grad = pl.pallas_call(
        kernel,
        out_shape=(vm((pages, wdev), F32), vm((width // (NX * NZ), width // NSEQ), F32)),
        in_specs=[any_] * 7,
        out_specs=(vmem, vmem),
        scratch_shapes=[
            vm((pages, wdev), I32),
            vm((pages, wdev), I32),
            pltpu.SMEM(counts.shape, I32),
            vm(flags.shape, I32),
            vm((pages, wdev, width), BF16),
            vm((pages, ppsz, width), BF16),
            vm((4, NX, width // NX, 256), BF16),
            vm((pages, NSEQ, cap, width), BF16),
            vm((pages, NSEQ, cap, width), BF16),
            vm((NSEQ, 2 * pages, wdev), I32),
            vm((NSEQ, pages, wdev), I32),
            vm((NSEQ, pages, wdev), F32),
            vm((width, width), F32),
            vm((pages, NSEQ * cap, ppsz), BF16),
            vm((pages, NSEQ * cap, 1), I32),
            vm((pages, NSEQ * cap, 1), F32),
            vm((pages, NSEQ * cap, 1), F32),
            vm((pages, NSEQ * cap, width), BF16),
            vm((NSEQ * cap, width), BF16),
            vm((NSEQ, pages, wdev), F32),
            vm((7, pages, wdev), F32),
            vm((NX, 256, half), BF16),
            vm((NX, 256, half), BF16),
            vm((NX, 256, half), F32),
            vm((3, NZ, 16, half), BF16),
            vm((2, NZ, 16, half), BF16),
            vm((2, NZ // 2, 16, half), BF16),
            vm((NZ, 16, half), F32),
            vm((2, 3, NX, NZ // 2, 16, 128), BF16),
            vm((2, 2, NX, NZ // 2, 16, 128), BF16),
            vm((2, NX, NZ // 2, 16, 128), BF16),
            vm((3, NZ, 16, 128), BF16),
            vm((3, NZ, 16, 128), BF16),
            vm((3, NZ, 16, 128), BF16),
            vm((3, NZ, 16, 128), BF16),
            vm((NZ, 32, 128), F32),
            vm((NZ, 32, 128), BF16),
            vm((7, 32, 128), BF16),
            dma((pages + 7,)),
        ]
        + [dma(shape) for shape in pairs for _ in range(2)],
        compiler_params=pltpu.CompilerParams(collective_id=1, has_side_effects=True, vmem_limit_bytes=56 << 20),
        name="grounding",
    )(words, patches, proj, routes.reshape(pages, wdev), targets, counts, flags)
    return pl.pallas_call(
        finish,
        out_shape=(jax.ShapeDtypeStruct(loss.shape, F32), jax.ShapeDtypeStruct(grad.shape, F32)),
        in_specs=[vmem, vmem],
        out_specs=(vmem, vmem),
        name="finish",
    )(pltpu.with_memory_space_constraint(loss, pltpu.VMEM), pltpu.with_memory_space_constraint(grad, pltpu.VMEM))


def solution(mesh):
    in_specs = (
        P("dp", "seq", None),
        P("dp", "seq", None),
        P("dp", None),
        P("dp", "seq", None),
        P("dp", "seq"),
        P("dp"),
        P("dp", None, None),
    )
    out_specs = (P("dp", "seq"), P("dp", "seq"))
    return jax.shard_map(local, mesh=mesh, in_specs=in_specs, out_specs=out_specs, check_vma=False)
```

```python
import functools
import math

import jax
import jax.numpy as jnp
from jax import lax
from jax.experimental import pallas as pl
from jax.experimental.pallas import tpu as pltpu
from jax.sharding import PartitionSpec as P

MESH = pl.DeviceIdType.MESH
NX, NY, NZ = 4, 4, 8
NSEQ = 8
BLOCK = 64
F32, BF16, I32 = jnp.float32, jnp.bfloat16, jnp.int32
PEERS = ((2, 0), (2, 1), (1, 0), (1, 1), (3, 0), (3, 1), (0, 1))
DXS = (2, 1, 3)
DYS = (2, 1, 3)
ZORDER = (4, 3, 5, 2, 6, 1, 7)
ZFAR = (4, 3, 5, 2, 6, 1, 7, 0)


def dot(a, b):
    return lax.dot_general(a, b, (((1,), (0,)), ((), ())), preferred_element_type=F32)


def dot_nt(a, b):
    return lax.dot_general(a, b, (((1,), (1,)), ((), ())), preferred_element_type=F32)


def dot_tn(a, b):
    return lax.dot_general(a, b, (((0,), (0,)), ((), ())), preferred_element_type=F32)


def iota(shape, dim):
    return lax.broadcasted_iota(I32, shape, dim)


def kernel(
    words_h, patches_h, proj_h, routes_h, targets_h, counts_h, flags_h,
    loss_o, grad_o,
    routes_r, targets_r, counts_s, flags_r, words_v, patches_v, proj_v, send_v, recv_v, meta_v, code_v, val_v,
    turned_v, grad_v, mask_v, tgt_v, coef_v, loss_v, dq_v, q_v, loss_s, loss_r,
    pair_s, pair_r, sum_v, a_s, a_r, ar_r, a_f, b_s, b_r, br_r, a2_s, a2_r, b2_s, b2_r, b_f, z3_f, z3_s, z3_r,
    loc_sem, disp_ss, disp_rs, meta_ss, meta_rs, aga_ss, aga_rs, agb_ss, agb_rs, sib_ss, sib_rs,
    loss_ss, loss_rs, pair_ss, pair_rs, a_ss, a_rs, ar_ss, ar_rs, b_ss, b_rs, br_ss, br_rs, a2_ss, a2_rs, b2_ss, b2_rs, z3_ss, z3_rs,
):
    pages, wdev, width = words_v.shape
    ppsz = patches_v.shape[1]
    cap = 2 * wdev // NSEQ
    scale = 2.0 / math.sqrt(width)
    d = lax.axis_index("dp")
    s = lax.axis_index("seq")
    x, z = d // NZ, d % NZ
    y, c = s // 2, s % 2

    def seq_of(dy, dc):
        return ((y + dy) % NY) * 2 + (c + dc) % 2

    def to_seq(dy, dc):
        return {"dp": d, "seq": seq_of(dy, dc)}

    def to_x(dx):
        return {"dp": ((x + dx) % NX) * NZ + z, "seq": s}

    def to_z(dz):
        return {"dp": x * NZ + (z + dz) % NZ, "seq": s}

    def remote(src, dst, ss, rs, dev):
        return pltpu.make_async_remote_copy(
            src_ref=src, dst_ref=dst, send_sem=ss, recv_sem=rs, device_id=dev, device_id_type=MESH
        )

    sent = []

    def go(cp):
        cp.start()
        sent.append(cp)
        return cp

    barrier = pltpu.get_barrier_semaphore()
    greet = [to_seq(*t) for t in PEERS] + [to_x(i) for i in DXS] + [to_z(i) for i in range(1, NZ)]
    for dev in greet:
        pl.semaphore_signal(barrier, inc=1, device_id=dev, device_id_type=MESH)

    rows = proj_h.shape[0]
    loads = [
        pltpu.make_async_copy(words_h.at[p], words_v.at[p], loc_sem.at[p]) for p in range(pages)
    ]
    for k in range(2):
        cols = pl.ds(pl.multiple_of((2 * c + k) * 256, 256), 256)
        loads.append(
            pltpu.make_async_copy(
                proj_h.at[:, cols],
                proj_v.at[2 * c + k, x, pl.ds(pl.multiple_of(z * rows, rows), rows)],
                loc_sem.at[pages + k],
            )
        )
    loads.append(pltpu.make_async_copy(patches_h, patches_v, loc_sem.at[pages + 2]))
    small = [
        pltpu.make_async_copy(src, dst, loc_sem.at[pages + 3 + i])
        for i, (src, dst) in enumerate(
            ((routes_h, routes_r), (targets_h, targets_r), (counts_h, counts_s), (flags_h, flags_r))
        )
    ]
    for cp in small + loads:
        cp.start()
    for cp in small:
        cp.wait()

    routes = routes_r[...]
    meta_v[s, 0:pages, :] = routes
    meta_v[s, pages : 2 * pages, :] = targets_r[...]
    upper = (iota((wdev, wdev), 0) < iota((wdev, wdev), 1)).astype(BF16)
    lanes = jnp.concatenate([jnp.broadcast_to(routes[p : p + 1, :], (NSEQ, wdev)) for p in range(pages)], axis=0)
    hot = lanes == iota((pages * NSEQ, wdev), 0) % NSEQ
    rank = jnp.where(hot, dot(hot.astype(F32).astype(BF16), upper), 0.0)

    def build(p):
        slot = jnp.sum(rank[p * NSEQ : (p + 1) * NSEQ], axis=0, keepdims=True).astype(I32)
        code = routes[p : p + 1, :] * cap + slot
        pick = (jnp.broadcast_to(code, (NSEQ * cap, wdev)) == iota((NSEQ * cap, wdev), 0)).astype(F32).astype(BF16)
        loads[p].wait()
        send_v[p] = dot(pick, words_v[p]).astype(BF16).reshape(NSEQ, cap, width)

    build(0)
    pl.semaphore_wait(barrier, len(greet))

    def dispatch(p, i):
        dy, dc = PEERS[i]
        return remote(
            send_v.at[p, seq_of(dy, dc)], recv_v.at[p, s], disp_ss.at[p, i], disp_rs.at[p, i], to_seq(dy, dc)
        )

    def send_page(p):
        for i in range(len(PEERS)):
            go(dispatch(p, i))

    def zrows(zb):
        return pl.ds(pl.multiple_of(zb * rows, rows), rows)

    half = rows * NZ // 2

    def ag_a(hop, i=0):
        if hop == 0:
            ref, dev = proj_v.at[2 * c, x, zrows(z)], to_z(i)
        elif hop == 1:
            ref, dev = proj_v.at[2 * c, x], to_x((1, 3)[i])
        else:
            ref, dev = proj_v.at[2 * c, (x + (3, 1)[i]) % NX, i * half : (i + 1) * half], to_x((1, 3)[i])
        at = i - 1 if hop == 0 else NZ - 1 + 2 * (hop - 1) + i
        return remote(ref, ref, aga_ss.at[at], aga_rs.at[at], dev)

    def ag_b(hop, i):
        if hop == 0:
            ref, dev = proj_v.at[2 * c + 1, x, zrows(z)], to_x(DXS[i])
        else:
            ref, dev = proj_v.at[2 * c + 1, :, zrows(z)], to_z(i)
        at = i if hop == 0 else 2 + i
        return remote(ref, ref, agb_ss.at[at], agb_rs.at[at], dev)

    def sib_a(dx):
        ref = proj_v.at[2 * c, (x + dx) % NX]
        return remote(ref, ref, sib_ss.at[dx], sib_rs.at[dx], to_seq(0, 1))

    def sib_b(i):
        ref = proj_v.at[2 * c + 1, :, zrows((z + i) % NZ)]
        return remote(ref, ref, sib_ss.at[NX + i], sib_rs.at[NX + i], to_seq(0, 1))

    meta_cp = []
    for i, (dy, dc) in enumerate(PEERS):
        meta_cp.append(go(remote(meta_v.at[s], meta_v.at[s], meta_ss.at[i], meta_rs.at[i], to_seq(dy, dc))))
    send_page(0)
    for i in range(2):
        loads[pages + i].wait()
    for i in range(3):
        go(ag_b(0, i))
    for i in range(1, NZ):
        go(ag_a(0, i))
    build(1)
    send_page(1)
    build(2)
    send_page(2)
    for i in range(3):
        ag_b(0, i).wait_recv()
    for i in ZORDER:
        go(ag_b(1, i))
    go(sib_b(0))
    build(3)
    send_page(3)
    for p in range(pages):
        recv_v[p, s] = send_v[p, s]
    for i in range(1, NZ):
        ag_a(0, i).wait_recv()
    for i in range(2):
        go(ag_a(1, i))
    go(sib_a(0))

    for cp in meta_cp:
        cp.wait_recv()
    for h in range(NSEQ):
        here = meta_v[h, 0:pages, :] == s
        rank = dot(here.astype(F32).astype(BF16), upper)
        code_v[h] = jnp.where(here, rank.astype(I32), -1)
        val_v[h] = (meta_v[h, pages : 2 * pages, :] + iota((pages, wdev), 1) * ppsz + 1).astype(F32)

    n_slots = NSEQ * cap
    spread = (iota((4 * NSEQ, ppsz), 0) == s * (ppsz // BLOCK) + iota((4 * NSEQ, ppsz), 1) // BLOCK).astype(F32).astype(BF16)
    home = iota((n_slots, 1), 0) // cap
    cand = iota((n_slots, ppsz), 1)

    def owned(p):
        return [
            jnp.broadcast_to(code_v[h, pl.ds(p, 1), :], (cap, wdev)) == iota((cap, wdev), 0) for h in range(NSEQ)
        ]

    def prepare(p):
        own = owned(p)
        val = jnp.concatenate(
            [
                jnp.sum(jnp.where(own[h], jnp.broadcast_to(val_v[h, pl.ds(p, 1), :], (cap, wdev)), 0.0), axis=1, keepdims=True)
                for h in range(NSEQ)
            ],
            axis=0,
        ).astype(I32)
        packed = jnp.maximum(val - 1, 0)
        tgt = packed % ppsz
        word = home * wdev + packed // ppsz
        hit = dot(
            (word // BLOCK == iota((n_slots, 2 * NSEQ), 1)).astype(F32).astype(BF16),
            dot(flags_r[p].astype(F32).astype(BF16), spread).astype(BF16),
        )
        allowed = (hit > 0.0) | (tgt // BLOCK == cand // BLOCK)
        mask_v[p] = allowed.astype(F32).astype(BF16)
        tgt_v[p] = tgt
        count = counts_s[p]
        valid = (val > 0) & (word < count)
        coef_v[p] = jnp.where(valid, 64.0 / jnp.full((n_slots, 1), count, I32).astype(F32), 0.0)

    for p in range(2):
        prepare(p)
    for i in range(2):
        ag_a(1, i).wait_recv()
    for i in range(2):
        go(ag_a(2, i))
    go(sib_a(1))
    go(sib_a(3))
    for i in ZORDER:
        ag_b(1, i).wait_recv()
        go(sib_b(NZ - i))
    for i in range(2):
        ag_a(2, i).wait_recv()
    go(sib_a(2))
    for p in range(2, pages):
        prepare(p)
    loads[pages + 2].wait()
    for i in range(NZ):
        sib_b(i).wait_recv()
    for i in range(NX):
        sib_a(i).wait_recv()

    def front(p, ahead=False):
        for i in range(len(PEERS)):
            dispatch(p, i).wait_recv()
        got = recv_v[p].reshape(n_slots, width)
        if ahead:
            turned_v[...] = got.T
            scores = dot_nt(got, q_v[...]) * scale
        else:
            for k in range(4):
                q_v[:, k * 256 : (k + 1) * 256] = dot(got, proj_v[k].reshape(width, 256)).astype(BF16)
            scores = dot_nt(q_v[...], patches_v[p]) * scale
        expo = jnp.where(mask_v[p].astype(F32) > 0.0, jnp.exp(scores), 0.0)
        total = jnp.sum(expo, axis=1, keepdims=True)
        is_t = cand == tgt_v[p]
        t_score = jnp.sum(jnp.where(is_t, scores, 0.0), axis=1, keepdims=True)
        coef = coef_v[p]
        loss_v[p] = jnp.where(coef > 0.0, jnp.log(total) - t_score, 0.0)
        dscore = (coef * (expo * (1.0 / total) - jnp.where(is_t, 1.0, 0.0))).astype(BF16)
        dq = (dot(dscore, patches_v[p]) * scale).astype(BF16)
        for j in range(NSEQ):
            at = ((j + c) % 2) * (width // 2) + (j // 2) * 128
            dq_v[p, :, pl.ds(pl.multiple_of(at, 128), 128)] = dq[:, j * 128 : (j + 1) * 128]

    def send_home(p):
        own, loss = owned(p), loss_v[p]
        for h in range(NSEQ):
            loss_s[h, pl.ds(p, 1), :] = jnp.sum(
                jnp.where(own[h], jnp.broadcast_to(loss[h * cap : (h + 1) * cap], (cap, wdev)), 0.0),
                axis=0,
                keepdims=True,
            )

    def page(p, carry):
        front(p)
        send_home(p)
        return carry

    last = pages - 1
    lax.fori_loop(0, last, page, 0)
    half = width // 2
    order = [(x + i) % NX for i in DXS] + [x]
    ats = [pl.ds(pl.multiple_of(xb * 256, 256), 256) for xb in order]

    def before(i):
        return dot_tn(
            recv_v[0:last, :, :, ats[i]].reshape(last * n_slots, 256), dq_v[0:last].reshape(last * n_slots, width)
        )

    for i in range(3):
        grad_v[i * 256 : (i + 1) * 256, :] = before(i)
    seen = dot_nt(patches_v[last, :, 0:256], proj_v[0].reshape(width, 256))
    for k in range(1, 4):
        seen = seen + dot_nt(patches_v[last, :, k * 256 : (k + 1) * 256], proj_v[k].reshape(width, 256))
    q_v[...] = seen.astype(BF16)
    front(last, True)

    n_early = len(sent)

    half = width // 2
    order = [(x + i) % NX for i in DXS] + [x]
    pair_cp = []
    for i, xb in enumerate(order):
        g = (grad_v[i * 256 : (i + 1) * 256, :] if i < 3 else before(i)) + dot(turned_v[ats[i], :], dq_v[last])
        pair_s[i] = g[:, half:].astype(BF16)
        pair_cp.append(go(remote(pair_s.at[i], pair_r.at[i], pair_ss.at[i], pair_rs.at[i], to_seq(0, 1))))
        sum_v[i] = g[:, :half]

    def ycols(dy):
        return pl.ds(pl.multiple_of(((y + dy) % NY) * 128, 128), 128)

    def part(i, which, cols=None):
        ref = sum_v[i] if cols is None else sum_v[i, :, cols]
        return ref.reshape(NZ, 2, 16, ref.shape[-1])[:, which]

    zh = NZ // 2
    halves = (slice(0, zh), slice(zh, NZ))
    step = (1, 3)
    ar_cp, ad_cp, br_cp, bd_cp = [None] * 2, [None] * 2, [], []
    for i in range(NX):
        pair_cp[i].wait_recv()
        sum_v[i] += pair_r[i].astype(F32)
        if i == 0:
            a_s[0] = part(0, 0).astype(BF16)
            for w in range(2):
                src = a_s.at[0, pl.ds(w * zh, zh)]
                ar_cp[w] = go(remote(src, ar_r.at[w], ar_ss.at[w], ar_rs.at[w], to_x(step[w])))
        elif i < 3:
            w = i - 1
            a_s[1 + w, halves[1 - w]] = part(i, 0)[halves[1 - w]].astype(BF16)
            at = pl.ds((1 - w) * zh, zh)
            ad_cp[w] = go(remote(a_s.at[1 + w, at], a_r.at[w, at], a_ss.at[w, 0], a_rs.at[w, 0], to_x(step[w])))
        far = part(i, 1, ycols(2)).astype(BF16)
        for w in range(2):
            b_s[w, 0, i] = far[halves[w]]
            b_s[w, 1, i] = part(i, 1, ycols(step[w]))[halves[1 - w]].astype(BF16)
            br_cp.append(go(remote(b_s.at[w, 0, i], br_r.at[w, i], br_ss.at[w, i], br_rs.at[w, i], to_seq(step[w], 0))))
            bd_cp.append(
                go(remote(b_s.at[w, 1, i], b_r.at[w, 0, i], b_ss.at[w, 0, i], b_rs.at[w, 0, i], to_seq(step[w], 0)))
            )
    am_cp, bm_cp = [], []
    for w in range(2):
        ar_cp[w].wait_recv()
        a_s[1 + w, halves[w]] = (part(1 + w, 0)[halves[w]] + ar_r[w].astype(F32)).astype(BF16)
        at = pl.ds(w * zh, zh)
        am_cp.append(go(remote(a_s.at[1 + w, at], a_r.at[w, at], a_ss.at[w, 1], a_rs.at[w, 1], to_x(step[w]))))
    for i in range(NX):
        for w in range(2):
            br_cp[2 * i + w].wait_recv()
            b_s[w, 2, i] = (part(i, 1, ycols(step[w]))[halves[w]] + br_r[w, i].astype(F32)).astype(BF16)
            bm_cp.append(
                go(remote(b_s.at[w, 2, i], b_r.at[w, 1, i], b_ss.at[w, 1, i], b_rs.at[w, 1, i], to_seq(step[w], 0)))
            )
    send_home(last)
    loss_cp = []
    for i, (dy, dc) in enumerate(PEERS):
        loss_cp.append(
            go(remote(loss_s.at[seq_of(dy, dc)], loss_r.at[i], loss_ss.at[i], loss_rs.at[i], to_seq(dy, dc)))
        )
    for cp in sent[:n_early]:
        cp.wait_send()
    for cp in ad_cp + am_cp:
        cp.wait_recv()
    a_f[...] = part(3, 0) + a_r[0].astype(F32) + a_r[1].astype(F32)
    a2_cp, b2_cp = [], []
    zs = [(z + r) % NZ for r in ZFAR]

    def by_half(src, dst, ss, rs, dev):
        return [
            go(remote(src.at[4 * u : 4 * u + 4], dst.at[4 * u : 4 * u + 4], ss.at[u], rs.at[u], dev)) for u in range(2)
        ]

    for j in range(3):
        for n, zb in enumerate(zs):
            a2_s[j, n] = a_f[zb, :, ycols(DYS[j])].astype(BF16)
        a2_cp.append(by_half(a2_s.at[j], a2_r.at[j], a2_ss.at[j], a2_rs.at[j], to_seq(DYS[j], 0)))
    for cp in bd_cp + bm_cp:
        cp.wait_recv()
    for i in range(NX):
        left = jnp.concatenate([b_r[0, 1, i], b_r[0, 0, i]], axis=0).astype(F32)
        right = jnp.concatenate([b_r[1, 0, i], b_r[1, 1, i]], axis=0).astype(F32)
        b_f[i] = part(i, 1, ycols(0)) + left + right
        if i < 3:
            for n, zb in enumerate(zs):
                b2_s[i, n] = b_f[i, zb].astype(BF16)
            b2_cp.append(by_half(b2_s.at[i], b2_r.at[i], b2_ss.at[i], b2_rs.at[i], to_x(DXS[i])))
    n_mid = len(sent)
    z3_cp = []
    for u in range(2):
        for cp in a2_cp + b2_cp:
            cp[u].wait_recv()
        for n in range(4 * u, 4 * u + 4):
            acc_a, acc_b = a_f[zs[n], :, ycols(0)], b_f[3, zs[n]]
            for j in range(3):
                acc_a = acc_a + a2_r[j, n].astype(F32)
                acc_b = acc_b + b2_r[j, n].astype(F32)
            if ZFAR[n] == 0:
                z3_f[0:16, :] = acc_a
                z3_f[16:32, :] = acc_b
            else:
                z3_s[n, 0:16, :] = acc_a.astype(BF16)
                z3_s[n, 16:32, :] = acc_b.astype(BF16)
                z3_cp.append(go(remote(z3_s.at[n], z3_r.at[n], z3_ss.at[n], z3_rs.at[n], to_z(ZFAR[n]))))
    for cp in loss_cp:
        cp.wait_recv()
    loss_o[...] = loss_s[s] + jnp.sum(loss_r[...], axis=0)
    for cp in sent[n_early:n_mid]:
        cp.wait_send()
    for cp in z3_cp:
        cp.wait_recv()
    grad_o[...] = z3_f[...] + jnp.sum(z3_r[...].astype(F32), axis=0)
    for cp in sent[n_mid:]:
        cp.wait_send()


def finish(loss_r, grad_r, loss_o, grad_o):
    loss_o[...] = loss_r[...]
    grad_o[...] = grad_r[...]


def local(words, patches, proj, routes, targets, counts, flags):
    pages, wdev, width = words.shape
    ppsz = patches.shape[1]
    cap = 2 * wdev // NSEQ
    half = width // 2
    vm = pltpu.VMEM
    dma = pltpu.SemaphoreType.DMA
    any_ = pl.BlockSpec(memory_space=pl.ANY)
    vmem = pl.BlockSpec(memory_space=pltpu.VMEM)
    pairs = [(pages, 7), (7,), (NZ + 3,), (NZ + 2,), (NX + NZ,), (7,), (4,), (2, 2), (2,), (2, 2, 4), (2, 4), (3, 2), (3, 2), (7,)]
    loss, grad = pl.pallas_call(
        kernel,
        out_shape=(vm((pages, wdev), F32), vm((width // (NX * NZ), width // NSEQ), F32)),
        in_specs=[any_] * 7,
        out_specs=(vmem, vmem),
        scratch_shapes=[
            vm((pages, wdev), I32),
            vm((pages, wdev), I32),
            pltpu.SMEM(counts.shape, I32),
            vm(flags.shape, I32),
            vm((pages, wdev, width), BF16),
            vm((pages, ppsz, width), BF16),
            vm((4, NX, width // NX, 256), BF16),
            vm((pages, NSEQ, cap, width), BF16),
            vm((pages, NSEQ, cap, width), BF16),
            vm((NSEQ, 2 * pages, wdev), I32),
            vm((NSEQ, pages, wdev), I32),
            vm((NSEQ, pages, wdev), F32),
            vm((width, NSEQ * cap), BF16),
            vm((width, width), F32),
            vm((pages, NSEQ * cap, ppsz), BF16),
            vm((pages, NSEQ * cap, 1), I32),
            vm((pages, NSEQ * cap, 1), F32),
            vm((pages, NSEQ * cap, 1), F32),
            vm((pages, NSEQ * cap, width), BF16),
            vm((NSEQ * cap, width), BF16),
            vm((NSEQ, pages, wdev), F32),
            vm((7, pages, wdev), F32),
            vm((NX, 256, half), BF16),
            vm((NX, 256, half), BF16),
            vm((NX, 256, half), F32),
            vm((3, NZ, 16, half), BF16),
            vm((2, NZ, 16, half), BF16),
            vm((2, NZ // 2, 16, half), BF16),
            vm((NZ, 16, half), F32),
            vm((2, 3, NX, NZ // 2, 16, 128), BF16),
            vm((2, 2, NX, NZ // 2, 16, 128), BF16),
            vm((2, NX, NZ // 2, 16, 128), BF16),
            vm((3, NZ, 16, 128), BF16),
            vm((3, NZ, 16, 128), BF16),
            vm((3, NZ, 16, 128), BF16),
            vm((3, NZ, 16, 128), BF16),
            vm((NX, NZ, 16, 128), F32),
            vm((32, 128), F32),
            vm((NZ, 32, 128), BF16),
            vm((7, 32, 128), BF16),
            dma((pages + 7,)),
        ]
        + [dma(shape) for shape in pairs for _ in range(2)],
        compiler_params=pltpu.CompilerParams(collective_id=1, has_side_effects=True, vmem_limit_bytes=56 << 20),
        name="grounding",
    )(words, patches, proj, routes.reshape(pages, wdev), targets, counts, flags)
    return pl.pallas_call(
        finish,
        out_shape=(jax.ShapeDtypeStruct(loss.shape, F32), jax.ShapeDtypeStruct(grad.shape, F32)),
        in_specs=[vmem, vmem],
        out_specs=(vmem, vmem),
        name="finish",
    )(pltpu.with_memory_space_constraint(loss, pltpu.VMEM), pltpu.with_memory_space_constraint(grad, pltpu.VMEM))


def solution(mesh):
    in_specs = (
        P("dp", "seq", None),
        P("dp", "seq", None),
        P("dp", None),
        P("dp", "seq", None),
        P("dp", "seq"),
        P("dp"),
        P("dp", None, None),
    )
    out_specs = (P("dp", "seq"), P("dp", "seq"))
    return jax.shard_map(local, mesh=mesh, in_specs=in_specs, out_specs=out_specs, check_vma=False)
```

```python
import functools
import math

import jax
import jax.numpy as jnp
from jax import lax
from jax.experimental import pallas as pl
from jax.experimental.pallas import tpu as pltpu
from jax.sharding import PartitionSpec as P

MESH = pl.DeviceIdType.MESH
NX, NY, NZ = 4, 4, 8
NSEQ = 8
BLOCK = 64
F32, BF16, I32 = jnp.float32, jnp.bfloat16, jnp.int32
PEERS = ((2, 0), (2, 1), (1, 0), (1, 1), (3, 0), (3, 1), (0, 1))
DXS = (2, 1, 3)
DYS = (2, 1, 3)
ZORDER = (4, 3, 5, 2, 6, 1, 7)
ZFAR = (4, 3, 5, 2, 6, 1, 7, 0)


def dot(a, b):
    return lax.dot_general(a, b, (((1,), (0,)), ((), ())), preferred_element_type=F32)


def dot_nt(a, b):
    return lax.dot_general(a, b, (((1,), (1,)), ((), ())), preferred_element_type=F32)


def dot_tn(a, b):
    return lax.dot_general(a, b, (((0,), (0,)), ((), ())), preferred_element_type=F32)


def iota(shape, dim):
    return lax.broadcasted_iota(I32, shape, dim)


def kernel(
    words_h, patches_h, proj_h, routes_h, targets_h, counts_h, flags_h,
    loss_o, grad_o,
    routes_r, targets_r, counts_s, flags_r, words_v, patches_v, proj_v, send_v, recv_v, meta_v, code_v, val_v,
    turned_v, grad_v, mask_v, tgt_v, coef_v, loss_v, dq_v, q_v, loss_s, loss_r,
    pair_s, pair_r, sum_v, a_s, a_r, ar_r, a_f, b_s, b_r, br_r, a2_s, a2_r, b2_s, b2_r, b_f, z3_f, z3_s, z3_r,
    loc_sem, disp_ss, disp_rs, meta_ss, meta_rs, aga_ss, aga_rs, agb_ss, agb_rs, sib_ss, sib_rs,
    loss_ss, loss_rs, pair_ss, pair_rs, a_ss, a_rs, ar_ss, ar_rs, b_ss, b_rs, br_ss, br_rs, a2_ss, a2_rs, b2_ss, b2_rs, z3_ss, z3_rs,
):
    pages, wdev, width = words_v.shape
    ppsz = patches_v.shape[1]
    cap = 2 * wdev // NSEQ
    scale = 2.0 / math.sqrt(width)
    d = lax.axis_index("dp")
    s = lax.axis_index("seq")
    x, z = d // NZ, d % NZ
    y, c = s // 2, s % 2

    def seq_of(dy, dc):
        return ((y + dy) % NY) * 2 + (c + dc) % 2

    def to_seq(dy, dc):
        return {"dp": d, "seq": seq_of(dy, dc)}

    def to_x(dx):
        return {"dp": ((x + dx) % NX) * NZ + z, "seq": s}

    def to_z(dz):
        return {"dp": x * NZ + (z + dz) % NZ, "seq": s}

    def remote(src, dst, ss, rs, dev):
        return pltpu.make_async_remote_copy(
            src_ref=src, dst_ref=dst, send_sem=ss, recv_sem=rs, device_id=dev, device_id_type=MESH
        )

    sent = []

    def go(cp):
        cp.start()
        sent.append(cp)
        return cp

    barrier = pltpu.get_barrier_semaphore()
    greet = [to_z(i) for i in ZORDER[:3]] + [to_seq(*t) for t in PEERS] + [to_z(i) for i in ZORDER[3:]] + [to_x(i) for i in DXS]
    for dev in greet:
        pl.semaphore_signal(barrier, inc=1, device_id=dev, device_id_type=MESH)

    rows = proj_h.shape[0]
    loads = [
        pltpu.make_async_copy(words_h.at[p], words_v.at[p], loc_sem.at[p]) for p in range(pages)
    ]
    for k in range(2):
        cols = pl.ds(pl.multiple_of((2 * c + k) * 256, 256), 256)
        loads.append(
            pltpu.make_async_copy(
                proj_h.at[:, cols],
                proj_v.at[2 * c + k, x, pl.ds(pl.multiple_of(z * rows, rows), rows)],
                loc_sem.at[pages + k],
            )
        )
    loads.append(pltpu.make_async_copy(patches_h, patches_v, loc_sem.at[pages + 2]))
    small = [
        pltpu.make_async_copy(src, dst, loc_sem.at[pages + 3 + i])
        for i, (src, dst) in enumerate(
            ((routes_h, routes_r), (targets_h, targets_r), (counts_h, counts_s), (flags_h, flags_r))
        )
    ]
    for cp in small + loads:
        cp.start()
    for cp in small:
        cp.wait()

    routes = routes_r[...]
    meta_v[s, 0:pages, :] = routes
    meta_v[s, pages : 2 * pages, :] = targets_r[...]
    upper = (iota((wdev, wdev), 0) < iota((wdev, wdev), 1)).astype(BF16)
    lanes = jnp.concatenate([jnp.broadcast_to(routes[p : p + 1, :], (NSEQ, wdev)) for p in range(pages)], axis=0)
    hot = lanes == iota((pages * NSEQ, wdev), 0) % NSEQ
    rank = jnp.where(hot, dot(hot.astype(F32).astype(BF16), upper), 0.0)

    def build(p):
        slot = jnp.sum(rank[p * NSEQ : (p + 1) * NSEQ], axis=0, keepdims=True).astype(I32)
        code = routes[p : p + 1, :] * cap + slot
        pick = (jnp.broadcast_to(code, (NSEQ * cap, wdev)) == iota((NSEQ * cap, wdev), 0)).astype(F32).astype(BF16)
        loads[p].wait()
        send_v[p] = dot(pick, words_v[p]).astype(BF16).reshape(NSEQ, cap, width)

    build(0)
    pl.semaphore_wait(barrier, len(greet))

    def dispatch(p, i):
        dy, dc = PEERS[i]
        return remote(
            send_v.at[p, seq_of(dy, dc)], recv_v.at[p, s], disp_ss.at[p, i], disp_rs.at[p, i], to_seq(dy, dc)
        )

    def send_page(p):
        for i in range(len(PEERS)):
            go(dispatch(p, i))

    def zrows(zb):
        return pl.ds(pl.multiple_of(zb * rows, rows), rows)

    half = rows * NZ // 2

    def ag_a(hop, i=0):
        if hop == 0:
            ref, dev = proj_v.at[2 * c, x, zrows(z)], to_z(i)
        elif hop == 1:
            ref, dev = proj_v.at[2 * c, x], to_x((1, 3)[i])
        else:
            ref, dev = proj_v.at[2 * c, (x + (3, 1)[i]) % NX, i * half : (i + 1) * half], to_x((1, 3)[i])
        at = i - 1 if hop == 0 else NZ - 1 + 2 * (hop - 1) + i
        return remote(ref, ref, aga_ss.at[at], aga_rs.at[at], dev)

    def ag_b(hop, i):
        if hop == 0:
            ref, dev = proj_v.at[2 * c + 1, x, zrows(z)], to_x(DXS[i])
        else:
            ref, dev = proj_v.at[2 * c + 1, :, zrows(z)], to_z(i)
        at = i if hop == 0 else 2 + i
        return remote(ref, ref, agb_ss.at[at], agb_rs.at[at], dev)

    def sib_a(dx):
        ref = proj_v.at[2 * c, (x + dx) % NX]
        return remote(ref, ref, sib_ss.at[dx], sib_rs.at[dx], to_seq(0, 1))

    def sib_b(i):
        ref = proj_v.at[2 * c + 1, :, zrows((z + i) % NZ)]
        return remote(ref, ref, sib_ss.at[NX + i], sib_rs.at[NX + i], to_seq(0, 1))

    send_page(0)
    for i in range(2):
        loads[pages + i].wait()
    for i in range(3):
        go(ag_b(0, i))
    for i in range(1, NZ):
        go(ag_a(0, i))
    meta_cp = []
    for i, (dy, dc) in enumerate(PEERS):
        meta_cp.append(go(remote(meta_v.at[s], meta_v.at[s], meta_ss.at[i], meta_rs.at[i], to_seq(dy, dc))))
    build(1)
    send_page(1)
    build(2)
    send_page(2)
    for i in range(3):
        ag_b(0, i).wait_recv()
    for i in ZORDER:
        go(ag_b(1, i))
    go(sib_b(0))
    build(3)
    send_page(3)
    for p in range(pages):
        recv_v[p, s] = send_v[p, s]
    for i in range(1, NZ):
        ag_a(0, i).wait_recv()
    for i in range(2):
        go(ag_a(1, i))
    go(sib_a(0))

    for cp in meta_cp:
        cp.wait_recv()
    for h in range(NSEQ):
        here = meta_v[h, 0:pages, :] == s
        rank = dot(here.astype(F32).astype(BF16), upper)
        code_v[h] = jnp.where(here, rank.astype(I32), -1)
        val_v[h] = (meta_v[h, pages : 2 * pages, :] + iota((pages, wdev), 1) * ppsz + 1).astype(F32)

    n_slots = NSEQ * cap
    spread = (iota((4 * NSEQ, ppsz), 0) == s * (ppsz // BLOCK) + iota((4 * NSEQ, ppsz), 1) // BLOCK).astype(F32).astype(BF16)
    home = iota((n_slots, 1), 0) // cap
    cand = iota((n_slots, ppsz), 1)

    def owned(p):
        return [
            jnp.broadcast_to(code_v[h, pl.ds(p, 1), :], (cap, wdev)) == iota((cap, wdev), 0) for h in range(NSEQ)
        ]

    def prepare(p):
        own = owned(p)
        val = jnp.concatenate(
            [
                jnp.sum(jnp.where(own[h], jnp.broadcast_to(val_v[h, pl.ds(p, 1), :], (cap, wdev)), 0.0), axis=1, keepdims=True)
                for h in range(NSEQ)
            ],
            axis=0,
        ).astype(I32)
        packed = jnp.maximum(val - 1, 0)
        tgt = packed % ppsz
        word = home * wdev + packed // ppsz
        hit = dot(
            (word // BLOCK == iota((n_slots, 2 * NSEQ), 1)).astype(F32).astype(BF16),
            dot(flags_r[p].astype(F32).astype(BF16), spread).astype(BF16),
        )
        allowed = (hit > 0.0) | (tgt // BLOCK == cand // BLOCK)
        mask_v[p] = allowed.astype(F32).astype(BF16)
        tgt_v[p] = tgt
        count = counts_s[p]
        valid = (val > 0) & (word < count)
        coef_v[p] = jnp.where(valid, 64.0 / jnp.full((n_slots, 1), count, I32).astype(F32), 0.0)

    for p in range(2):
        prepare(p)
    for i in range(2):
        ag_a(1, i).wait_recv()
    for i in range(2):
        go(ag_a(2, i))
    go(sib_a(1))
    go(sib_a(3))
    for i in ZORDER:
        ag_b(1, i).wait_recv()
        go(sib_b(NZ - i))
    for i in range(2):
        ag_a(2, i).wait_recv()
    go(sib_a(2))
    for p in range(2, pages):
        prepare(p)
    loads[pages + 2].wait()
    for i in range(NZ):
        sib_b(i).wait_recv()
    for i in range(NX):
        sib_a(i).wait_recv()

    def front(p, ahead=False):
        for i in range(len(PEERS)):
            dispatch(p, i).wait_recv()
        got = recv_v[p].reshape(n_slots, width)
        if ahead:
            turned_v[...] = got.T
            scores = dot_nt(got, q_v[...]) * scale
        else:
            for k in range(4):
                q_v[:, k * 256 : (k + 1) * 256] = dot(got, proj_v[k].reshape(width, 256)).astype(BF16)
            scores = dot_nt(q_v[...], patches_v[p]) * scale
        expo = jnp.where(mask_v[p].astype(F32) > 0.0, jnp.exp(scores), 0.0)
        total = jnp.sum(expo, axis=1, keepdims=True)
        is_t = cand == tgt_v[p]
        t_score = jnp.sum(jnp.where(is_t, scores, 0.0), axis=1, keepdims=True)
        coef = coef_v[p]
        loss_v[p] = jnp.where(coef > 0.0, jnp.log(total) - t_score, 0.0)
        dscore = (coef * (expo * (1.0 / total) - jnp.where(is_t, 1.0, 0.0))).astype(BF16)
        dq = (dot(dscore, patches_v[p]) * scale).astype(BF16)
        for j in range(NSEQ):
            at = ((j + c) % 2) * (width // 2) + (j // 2) * 128
            dq_v[p, :, pl.ds(pl.multiple_of(at, 128), 128)] = dq[:, j * 128 : (j + 1) * 128]

    def send_home(p):
        own, loss = owned(p), loss_v[p]
        for h in range(NSEQ):
            loss_s[h, pl.ds(p, 1), :] = jnp.sum(
                jnp.where(own[h], jnp.broadcast_to(loss[h * cap : (h + 1) * cap], (cap, wdev)), 0.0),
                axis=0,
                keepdims=True,
            )

    def page(p, carry):
        front(p)
        send_home(p)
        return carry

    last = pages - 1
    lax.fori_loop(0, last, page, 0)
    half = width // 2
    order = [(x + i) % NX for i in DXS] + [x]
    ats = [pl.ds(pl.multiple_of(xb * 256, 256), 256) for xb in order]

    def before(i):
        return dot_tn(
            recv_v[0:last, :, :, ats[i]].reshape(last * n_slots, 256), dq_v[0:last].reshape(last * n_slots, width)
        )

    for i in range(3):
        grad_v[i * 256 : (i + 1) * 256, :] = before(i)
    seen = dot_nt(patches_v[last, :, 0:256], proj_v[0].reshape(width, 256))
    for k in range(1, 4):
        seen = seen + dot_nt(patches_v[last, :, k * 256 : (k + 1) * 256], proj_v[k].reshape(width, 256))
    q_v[...] = seen.astype(BF16)
    front(last, True)

    n_early = len(sent)

    half = width // 2
    order = [(x + i) % NX for i in DXS] + [x]
    pair_cp = []
    for i, xb in enumerate(order):
        g = (grad_v[i * 256 : (i + 1) * 256, :] if i < 3 else before(i)) + dot(turned_v[ats[i], :], dq_v[last])
        pair_s[i] = g[:, half:].astype(BF16)
        pair_cp.append(go(remote(pair_s.at[i], pair_r.at[i], pair_ss.at[i], pair_rs.at[i], to_seq(0, 1))))
        sum_v[i] = g[:, :half]

    def ycols(dy):
        return pl.ds(pl.multiple_of(((y + dy) % NY) * 128, 128), 128)

    def part(i, which, cols=None):
        ref = sum_v[i] if cols is None else sum_v[i, :, cols]
        return ref.reshape(NZ, 2, 16, ref.shape[-1])[:, which]

    zh = NZ // 2
    halves = (slice(0, zh), slice(zh, NZ))
    step = (1, 3)
    ar_cp, ad_cp, br_cp, bd_cp = [None] * 2, [None] * 2, [], []
    for i in range(NX):
        pair_cp[i].wait_recv()
        sum_v[i] += pair_r[i].astype(F32)
        if i == 0:
            a_s[0] = part(0, 0).astype(BF16)
            for w in range(2):
                src = a_s.at[0, pl.ds(w * zh, zh)]
                ar_cp[w] = go(remote(src, ar_r.at[w], ar_ss.at[w], ar_rs.at[w], to_x(step[w])))
        elif i < 3:
            w = i - 1
            a_s[1 + w, halves[1 - w]] = part(i, 0)[halves[1 - w]].astype(BF16)
            at = pl.ds((1 - w) * zh, zh)
            ad_cp[w] = go(remote(a_s.at[1 + w, at], a_r.at[w, at], a_ss.at[w, 0], a_rs.at[w, 0], to_x(step[w])))
        far = part(i, 1, ycols(2)).astype(BF16)
        for w in range(2):
            b_s[w, 0, i] = far[halves[w]]
            b_s[w, 1, i] = part(i, 1, ycols(step[w]))[halves[1 - w]].astype(BF16)
            br_cp.append(go(remote(b_s.at[w, 0, i], br_r.at[w, i], br_ss.at[w, i], br_rs.at[w, i], to_seq(step[w], 0))))
            bd_cp.append(
                go(remote(b_s.at[w, 1, i], b_r.at[w, 0, i], b_ss.at[w, 0, i], b_rs.at[w, 0, i], to_seq(step[w], 0)))
            )
    am_cp, bm_cp = [], []
    for w in range(2):
        ar_cp[w].wait_recv()
        a_s[1 + w, halves[w]] = (part(1 + w, 0)[halves[w]] + ar_r[w].astype(F32)).astype(BF16)
        at = pl.ds(w * zh, zh)
        am_cp.append(go(remote(a_s.at[1 + w, at], a_r.at[w, at], a_ss.at[w, 1], a_rs.at[w, 1], to_x(step[w]))))
    for i in range(NX):
        for w in range(2):
            br_cp[2 * i + w].wait_recv()
            b_s[w, 2, i] = (part(i, 1, ycols(step[w]))[halves[w]] + br_r[w, i].astype(F32)).astype(BF16)
            bm_cp.append(
                go(remote(b_s.at[w, 2, i], b_r.at[w, 1, i], b_ss.at[w, 1, i], b_rs.at[w, 1, i], to_seq(step[w], 0)))
            )
    send_home(last)
    loss_cp = []
    for i, (dy, dc) in enumerate(PEERS):
        loss_cp.append(
            go(remote(loss_s.at[seq_of(dy, dc)], loss_r.at[i], loss_ss.at[i], loss_rs.at[i], to_seq(dy, dc)))
        )
    for cp in sent[:n_early]:
        cp.wait_send()
    for cp in ad_cp + am_cp:
        cp.wait_recv()
    a_f[...] = part(3, 0) + a_r[0].astype(F32) + a_r[1].astype(F32)
    a2_cp, b2_cp = [], []
    zs = [(z + r) % NZ for r in ZFAR]

    def by_half(src, dst, ss, rs, dev):
        return [
            go(remote(src.at[4 * u : 4 * u + 4], dst.at[4 * u : 4 * u + 4], ss.at[u], rs.at[u], dev)) for u in range(2)
        ]

    for j in range(3):
        for n, zb in enumerate(zs):
            a2_s[j, n] = a_f[zb, :, ycols(DYS[j])].astype(BF16)
        a2_cp.append(by_half(a2_s.at[j], a2_r.at[j], a2_ss.at[j], a2_rs.at[j], to_seq(DYS[j], 0)))
    for cp in bd_cp + bm_cp:
        cp.wait_recv()
    for i in range(NX):
        left = jnp.concatenate([b_r[0, 1, i], b_r[0, 0, i]], axis=0).astype(F32)
        right = jnp.concatenate([b_r[1, 0, i], b_r[1, 1, i]], axis=0).astype(F32)
        b_f[i] = part(i, 1, ycols(0)) + left + right
        if i < 3:
            for n, zb in enumerate(zs):
                b2_s[i, n] = b_f[i, zb].astype(BF16)
            b2_cp.append(by_half(b2_s.at[i], b2_r.at[i], b2_ss.at[i], b2_rs.at[i], to_x(DXS[i])))
    n_mid = len(sent)
    z3_cp = []
    for u in range(2):
        for cp in a2_cp + b2_cp:
            cp[u].wait_recv()
        for n in range(4 * u, 4 * u + 4):
            acc_a, acc_b = a_f[zs[n], :, ycols(0)], b_f[3, zs[n]]
            for j in range(3):
                acc_a = acc_a + a2_r[j, n].astype(F32)
                acc_b = acc_b + b2_r[j, n].astype(F32)
            if ZFAR[n] == 0:
                z3_f[0:16, :] = acc_a
                z3_f[16:32, :] = acc_b
            else:
                z3_s[n, 0:16, :] = acc_a.astype(BF16)
                z3_s[n, 16:32, :] = acc_b.astype(BF16)
                z3_cp.append(go(remote(z3_s.at[n], z3_r.at[n], z3_ss.at[n], z3_rs.at[n], to_z(ZFAR[n]))))
    for cp in loss_cp:
        cp.wait_recv()
    loss_o[...] = loss_s[s] + jnp.sum(loss_r[...], axis=0)
    for cp in sent[n_early:n_mid]:
        cp.wait_send()
    for cp in z3_cp:
        cp.wait_recv()
    grad_o[...] = z3_f[...] + jnp.sum(z3_r[...].astype(F32), axis=0)
    for cp in sent[n_mid:]:
        cp.wait_send()


def finish(loss_r, grad_r, loss_o, grad_o):
    loss_o[...] = loss_r[...]
    grad_o[...] = grad_r[...]


def local(words, patches, proj, routes, targets, counts, flags):
    pages, wdev, width = words.shape
    ppsz = patches.shape[1]
    cap = 2 * wdev // NSEQ
    half = width // 2
    vm = pltpu.VMEM
    dma = pltpu.SemaphoreType.DMA
    any_ = pl.BlockSpec(memory_space=pl.ANY)
    vmem = pl.BlockSpec(memory_space=pltpu.VMEM)
    pairs = [(pages, 7), (7,), (NZ + 3,), (NZ + 2,), (NX + NZ,), (7,), (4,), (2, 2), (2,), (2, 2, 4), (2, 4), (3, 2), (3, 2), (7,)]
    loss, grad = pl.pallas_call(
        kernel,
        out_shape=(vm((pages, wdev), F32), vm((width // (NX * NZ), width // NSEQ), F32)),
        in_specs=[any_] * 7,
        out_specs=(vmem, vmem),
        scratch_shapes=[
            vm((pages, wdev), I32),
            vm((pages, wdev), I32),
            pltpu.SMEM(counts.shape, I32),
            vm(flags.shape, I32),
            vm((pages, wdev, width), BF16),
            vm((pages, ppsz, width), BF16),
            vm((4, NX, width // NX, 256), BF16),
            vm((pages, NSEQ, cap, width), BF16),
            vm((pages, NSEQ, cap, width), BF16),
            vm((NSEQ, 2 * pages, wdev), I32),
            vm((NSEQ, pages, wdev), I32),
            vm((NSEQ, pages, wdev), F32),
            vm((width, NSEQ * cap), BF16),
            vm((width, width), F32),
            vm((pages, NSEQ * cap, ppsz), BF16),
            vm((pages, NSEQ * cap, 1), I32),
            vm((pages, NSEQ * cap, 1), F32),
            vm((pages, NSEQ * cap, 1), F32),
            vm((pages, NSEQ * cap, width), BF16),
            vm((NSEQ * cap, width), BF16),
            vm((NSEQ, pages, wdev), F32),
            vm((7, pages, wdev), F32),
            vm((NX, 256, half), BF16),
            vm((NX, 256, half), BF16),
            vm((NX, 256, half), F32),
            vm((3, NZ, 16, half), BF16),
            vm((2, NZ, 16, half), BF16),
            vm((2, NZ // 2, 16, half), BF16),
            vm((NZ, 16, half), F32),
            vm((2, 3, NX, NZ // 2, 16, 128), BF16),
            vm((2, 2, NX, NZ // 2, 16, 128), BF16),
            vm((2, NX, NZ // 2, 16, 128), BF16),
            vm((3, NZ, 16, 128), BF16),
            vm((3, NZ, 16, 128), BF16),
            vm((3, NZ, 16, 128), BF16),
            vm((3, NZ, 16, 128), BF16),
            vm((NX, NZ, 16, 128), F32),
            vm((32, 128), F32),
            vm((NZ, 32, 128), BF16),
            vm((7, 32, 128), BF16),
            dma((pages + 7,)),
        ]
        + [dma(shape) for shape in pairs for _ in range(2)],
        compiler_params=pltpu.CompilerParams(collective_id=1, has_side_effects=True, vmem_limit_bytes=56 << 20),
        name="grounding",
    )(words, patches, proj, routes.reshape(pages, wdev), targets, counts, flags)
    return pl.pallas_call(
        finish,
        out_shape=(jax.ShapeDtypeStruct(loss.shape, F32), jax.ShapeDtypeStruct(grad.shape, F32)),
        in_specs=[vmem, vmem],
        out_specs=(vmem, vmem),
        name="finish",
    )(pltpu.with_memory_space_constraint(loss, pltpu.VMEM), pltpu.with_memory_space_constraint(grad, pltpu.VMEM))


def solution(mesh):
    in_specs = (
        P("dp", "seq", None),
        P("dp", "seq", None),
        P("dp", None),
        P("dp", "seq", None),
        P("dp", "seq"),
        P("dp"),
        P("dp", None, None),
    )
    out_specs = (P("dp", "seq"), P("dp", "seq"))
    return jax.shard_map(local, mesh=mesh, in_specs=in_specs, out_specs=out_specs, check_vma=False)
```
